32 devices in a mesh: member: 2 (over y), lat: 4 (over z), lev: 2 (over x), fld: 2 (over core).
Axes of the slice: x: 2, y: 2, z: 4, core: 2. Of those that a mesh axis runs over, the one named last changes fastest.
Arguments:
- tracer: bfloat16 [8, 800, 1600], P('member', 'lat', ('lev', 'fld')), parts along dimension 0, may hold values from -6 to 6
- wind_east: bfloat16 [8, 800, 1600], P('member', 'lat', ('lev', 'fld')), parts along dimension 0, may hold values from -3 to 3
- wind_north: bfloat16 [8, 800, 1600], P('member', 'lat', ('lev', 'fld')), parts along dimension 0, may hold values from -3 to 3
- keep_m: int32 [800], P('lat'), may hold values from 9 to 400, as said below
- slot_wave: int32 [400], replicated, may hold values from 0 to 399, each once
Outputs:
- spectral: float32 [8, 400, 2, 400], P(('member', 'lev', 'fld'), 'lat'), parts along dimension 0
The draws below stay inside these ranges and needn't reach their ends.
There are 2 independent parts, one for each index of `member`. The reference program is written for one: setup_inputs(seed, part) draws one part's arguments, and reference() takes and returns one part's arrays. A program takes and returns all parts, laid end to end along the dimension named above; an argument that names none is the same for every part. Nothing has to cross between parts.
Inputs may be any that keep to these rules, and one draw needn't show every extreme that they name: keep_m equals 400 at rows 399 and 400, and 9 at rows 0 and 799. Slot s of the output holds wavenumber slot_wave[s]; values of 400 or more mark empty slots.
All inputs are finite; a program needn't handle non-finite values.
Results may differ from the reference program's by a relative error of at most 0.0003.
Values may be sent and summed in bfloat16 or wider, within the bound.
A program may use at most 64 MiB of HBM per device.

```python
import math
import jax
import jax.numpy as jnp
from jax import lax

M = 400
LEV = 4
NLAT = 800
NLON = 1600
MSLOT = 400


def draw_keep_m(key, part):
    row_index = jnp.arange(NLAT, dtype=jnp.int32)
    distance = jnp.minimum(row_index, NLAT - 1 - row_index)
    jitter = jax.random.randint(key, (NLAT,), 0, M // 8 + 1, dtype=jnp.int32)
    jitter = jnp.where(distance > 0, jitter, 0)
    return jnp.minimum(M, 9 + distance + jitter).astype(jnp.int32)


def shard_levels(rng, shape, pieces, low, top_value):
    factor_of, own = 1.0, jax.random.fold_in(rng, 6)
    for position, parts in pieces:
        steps = jnp.exp(jax.random.uniform(jax.random.fold_in(own, position), (parts,), jnp.float32, low / len(pieces), top_value / len(pieces)))
        factor_of = factor_of * jnp.repeat(steps, shape[position] // parts).reshape([-1 if axis == position else 1 for axis in range(len(shape))])
    return factor_of


def noise(key, shape, scale, reach, split=(), held_as=jnp.bfloat16):
    values = scale * jax.random.normal(key, shape, jnp.float32)
    if split:
        values = values * shard_levels(key, shape, split, -0.22, 0.18)
    return jnp.clip(values, -reach, reach).astype(held_as)


def setup_inputs(seed: int = 0, part: int = 0) -> dict:
    splits = jax.random.split(jax.random.key(seed), 6)
    part_keys = jax.random.split(jax.random.fold_in(splits[5], part), 6)
    return {
        "tracer": noise(part_keys[0], (LEV, NLAT, NLON), 1.0, 6.0, ((1, 4), (2, 4))),
        "wind_east": noise(part_keys[1], (LEV, NLAT, NLON), 0.5, 3.0, ((1, 4), (2, 4))),
        "wind_north": noise(part_keys[2], (LEV, NLAT, NLON), 0.5, 3.0, ((1, 4), (2, 4))),
        "keep_m": draw_keep_m(jax.random.fold_in(splits[5], 71), part),
        "slot_wave": jax.random.permutation(splits[4], MSLOT).astype(jnp.int32),
    }


precise = lax.Precision.HIGHEST
block_rows = 16

def fourier_table(wave_ids, lon_count):
    grid_index = jnp.arange(lon_count, dtype=jnp.int32)
    phase_index = wave_ids.astype(jnp.int32)[:, None] * grid_index[None, :] % lon_count
    angles = 2.0 * math.pi / lon_count * phase_index.astype(jnp.float32)
    factor = 1.0 / math.sqrt(lon_count)
    return jnp.stack([jnp.cos(angles), -jnp.sin(angles)], axis=1) * factor

def advect(padded, east_wind, north_wind, first_row, lat_total):
    rows_here = padded.shape[1] - 2
    row_ids = first_row - 1 + jnp.arange(rows_here + 2, dtype=jnp.int32)
    inside = ((row_ids >= 0) & (row_ids < lat_total)).astype(jnp.float32)
    field_rows = padded.astype(jnp.float32) * inside[None, :, None]
    centre = field_rows[:, 1:-1, 1:-1]
    east_diff = field_rows[:, 1:-1, 2:] - field_rows[:, 1:-1, :-2]
    north_diff = field_rows[:, 2:, 1:-1] - field_rows[:, :-2, 1:-1]
    return centre - 0.5 * east_wind.astype(jnp.float32) * east_diff - 0.5 * north_wind.astype(jnp.float32) * north_diff

def legendre_setup(wave_ids, trunc_count, lat_total, lat_used):
    degree = jnp.minimum(wave_ids, trunc_count - 1).astype(jnp.float32)
    counter = jnp.arange(1, trunc_count, dtype=jnp.float32)
    log_terms = jnp.log1p(0.5 / counter)
    log_norm = lax.optimization_barrier(jnp.sum(jnp.where(counter[None, :] <= degree[:, None], log_terms[None, :], 0.0), axis=1))
    colatitude = math.pi / lat_total * (jnp.arange(lat_used, dtype=jnp.float32) + 0.5)
    sine_rows = jnp.sin(colatitude)
    cosines = jnp.cos(colatitude)
    start_log = 0.5 * (log_norm[:, None] - math.log(2.0)) + degree[:, None] * jnp.log(sine_rows)[None, :]
    return (degree, cosines, start_log)

def legendre_rows(recurrence, degree, cosines, first_order):
    before, current, log_scale = recurrence
    rows_list = [current]
    for offset in range(1, block_rows + 1):
        order_value = (first_order + offset).astype(jnp.float32)
        total_degree = degree[:, None] + order_value
        growth = jnp.sqrt((4.0 * total_degree * total_degree - 1.0) / (total_degree * total_degree - degree[:, None] * degree[:, None]))
        lower_degree = total_degree - 1.0
        damping = jnp.sqrt((lower_degree * lower_degree - degree[:, None] * degree[:, None]) / jnp.maximum(4.0 * lower_degree * lower_degree - 1.0, 1.0))
        advanced = growth * (cosines[None, :] * current - damping * before)
        before, current = (current, advanced)
        if offset < block_rows:
            rows_list.append(current)
    biggest = jnp.maximum(jnp.abs(before), jnp.abs(current))
    table_rows = jnp.stack(rows_list, axis=1) * jnp.exp(log_scale)[:, None, :]
    return (table_rows, (before / biggest, current / biggest, log_scale + jnp.log(biggest)))

def legendre_sweep(legendre_basis, contract, level_count, trunc_count):
    degree, cosines, start_log = legendre_basis
    slot_count = degree.shape[0]
    lat_used = cosines.shape[0]
    before = jnp.zeros((slot_count, lat_used), jnp.float32)
    current = jnp.ones((slot_count, lat_used), jnp.float32)
    result_init = jnp.zeros((level_count, slot_count, 2, trunc_count), jnp.float32)

    def advance(block_index, loop_carry):
        recurrence, result_now = loop_carry
        first_order = block_index * block_rows
        table_rows, recurrence = legendre_rows(recurrence, degree, cosines, first_order)
        orders = (first_order + jnp.arange(block_rows, dtype=jnp.int32)).astype(jnp.float32)
        inside_triangle = (orders[None, :] < trunc_count - degree[:, None]).astype(jnp.float32)
        partial_value = contract(table_rows * inside_triangle[:, :, None])
        result_now = lax.dynamic_update_slice_in_dim(result_now, partial_value, first_order, 3)
        return (recurrence, result_now)
    finished = lax.fori_loop(0, trunc_count // block_rows, advance, ((before, current, start_log), result_init))
    return finished[1]

def reference(tracer, wind_east, wind_north, keep_m, slot_wave):
    fourier_matrix = fourier_table(slot_wave, NLON)

    def one_level(level_args):
        tracer_row, east_row, north_row = level_args
        padded = jnp.pad(tracer_row[None], ((0, 0), (1, 1), (1, 1)), mode='wrap')
        advected = advect(padded, east_row[None], north_row[None], 0, NLAT)[0]
        return jnp.einsum('sck,jk->scj', fourier_matrix, advected, precision=precise)
    fourier = lax.map(one_level, (tracer, wind_east, wind_north))
    kept_mask = (slot_wave[:, None] < keep_m[None, :]).astype(jnp.float32)
    fourier = fourier * kept_mask[None, :, None, :]
    spectral_in = jnp.transpose(fourier, (1, 2, 0, 3))
    sines_all = jnp.sin(math.pi / NLAT * (jnp.arange(NLAT, dtype=jnp.float32) + 0.5))
    weighted = spectral_in * (sines_all * math.sqrt(2.0 / NLAT))[None, None, None, :]
    legendre_basis = legendre_setup(slot_wave, M, NLAT, NLAT)

    def contract(table_rows):
        return jnp.einsum('stj,scij->isct', table_rows, weighted, precision=precise)
    return legendre_sweep(legendre_basis, contract, LEV, M)
```

```python
import math

import jax
import jax.numpy as jnp
from jax import lax
from jax.experimental import pallas as pl
from jax.experimental.pallas import tpu as pltpu
from jax.sharding import PartitionSpec as P

M = 400
NLAT = 800
NLON = 1600

block_rows = 16
slot_tile = 16
GROUP = ("lev", "fld")


def round_up(value, multiple):
    return -(-value // multiple) * multiple


def edges(block, axis, dim):
    count = lax.axis_size(axis)
    forward = [(i, (i + 1) % count) for i in range(count)]
    backward = [(target, source) for source, target in forward]
    low = lax.ppermute(
        lax.slice_in_dim(block, block.shape[dim] - 1, None, axis=dim), axis, forward
    )
    high = lax.ppermute(lax.slice_in_dim(block, 0, 1, axis=dim), axis, backward)
    return low, high


def fourier_table(wave_ids, lon_count):
    grid_index = jnp.arange(lon_count, dtype=jnp.int32)
    phase_index = wave_ids[:, None] * grid_index[None, :] % lon_count
    angles = 2.0 * math.pi / lon_count * phase_index.astype(jnp.float32)
    factor = 1.0 / math.sqrt(lon_count)
    return jnp.stack([jnp.cos(angles), -jnp.sin(angles)], axis=1) * factor


def advect(tracer, east_wind, north_wind, first_row, lat_total):
    west, east = edges(tracer, GROUP, 2)
    above, below = edges(tracer, "lat", 1)
    centre = tracer.astype(jnp.float32)
    rows_here = tracer.shape[1]
    has_above = (first_row > 0).astype(jnp.float32)
    has_below = (first_row + rows_here < lat_total).astype(jnp.float32)
    above = above.astype(jnp.float32) * has_above
    below = below.astype(jnp.float32) * has_below
    east_diff = jnp.concatenate(
        [centre[:, :, 1:], east.astype(jnp.float32)], axis=2
    ) - jnp.concatenate([west.astype(jnp.float32), centre[:, :, :-1]], axis=2)
    north_diff = jnp.concatenate([centre[:, 1:], below], axis=1) - jnp.concatenate(
        [above, centre[:, :-1]], axis=1
    )
    return (
        centre
        - 0.5 * east_wind.astype(jnp.float32) * east_diff
        - 0.5 * north_wind.astype(jnp.float32) * north_diff
    )


def legendre_setup(wave_ids, trunc_count, lat_total, lat_used, lat_padded):
    degree = jnp.minimum(wave_ids, trunc_count - 1).astype(jnp.float32)
    counter = jnp.arange(1, trunc_count, dtype=jnp.float32)
    log_terms = jnp.log1p(0.5 / counter)
    log_norm = jnp.sum(
        jnp.where(counter[None, :] <= degree[:, None], log_terms[None, :], 0.0), axis=1
    )
    rows = jnp.minimum(jnp.arange(lat_padded), lat_used - 1)
    colatitude = math.pi / lat_total * (rows.astype(jnp.float32) + 0.5)
    start_log = 0.5 * (log_norm[:, None] - math.log(2.0)) + degree[:, None] * jnp.log(
        jnp.sin(colatitude)
    )
    orders = jnp.arange(1, trunc_count + 1, dtype=jnp.float32)
    total = degree[:, None] + orders
    square = degree[:, None] * degree[:, None]
    growth = jnp.sqrt((4.0 * total * total - 1.0) / (total * total - square))
    lower = total - 1.0
    damping = jnp.sqrt(
        (lower * lower - square) / jnp.maximum(4.0 * lower * lower - 1.0, 1.0)
    )

    def blocked(values):
        return values.reshape(values.shape[0], -1, block_rows).transpose(1, 0, 2)

    return blocked(growth), blocked(damping), jnp.cos(colatitude)[None, :], start_log


def table_kernel(growth_ref, damping_ref, cosine_ref, start_ref, high_ref, low_ref):
    cosine = cosine_ref[...]
    shape = start_ref.shape

    def advance(index, carry):
        before, current, log_scale = carry
        scale = jnp.exp(log_scale)
        growth = growth_ref[index]
        damping = damping_ref[index]
        for offset in range(block_rows):
            row = current * scale
            high = row.astype(jnp.bfloat16)
            low = (row - high.astype(jnp.float32)).astype(jnp.bfloat16)
            place = index * (block_rows // 2) + offset // 2
            high_ref[offset % 2, place] = high
            low_ref[offset % 2, place] = low
            advanced = growth[:, offset : offset + 1] * (
                cosine * current - damping[:, offset : offset + 1] * before
            )
            before, current = current, advanced
        biggest = jnp.maximum(jnp.abs(before), jnp.abs(current))
        return before / biggest, current / biggest, log_scale + jnp.log(biggest)

    lax.fori_loop(
        0,
        growth_ref.shape[0],
        advance,
        (jnp.zeros(shape, jnp.float32), jnp.ones(shape, jnp.float32), start_ref[...]),
    )


def legendre_table(growth, damping, cosine, start_log):
    blocks, slots, _ = growth.shape
    lats = cosine.shape[1]
    half = blocks * block_rows // 2
    out = jax.ShapeDtypeStruct((2, half, slots, lats), jnp.bfloat16)
    coef_spec = pl.BlockSpec((blocks, slot_tile, block_rows), lambda i: (0, i, 0))
    out_spec = pl.BlockSpec((2, half, slot_tile, lats), lambda i: (0, 0, i, 0))
    size = 2 * half * slots * lats
    return pl.pallas_call(
        table_kernel,
        grid=(slots // slot_tile,),
        in_specs=[
            coef_spec,
            coef_spec,
            pl.BlockSpec((1, lats), lambda i: (0, 0)),
            pl.BlockSpec((slot_tile, lats), lambda i: (i, 0)),
        ],
        out_specs=[out_spec, out_spec],
        out_shape=[out, out],
        cost_estimate=pl.CostEstimate(
            flops=10 * size, bytes_accessed=4 * size, transcendentals=size // 4
        ),
        name="legendre_table",
    )(growth, damping, cosine, start_log)


def contract_kernel(columns_per_slot, high_ref, low_ref, weight_high_ref, weight_low_ref, out_ref):
    _, orders, slots, lats = high_ref.shape
    columns = out_ref.shape[2]
    high = high_ref[0].reshape(orders * slots, lats)
    low = low_ref[0].reshape(orders * slots, lats)

    def dot(left, right):
        return lax.dot_general(
            left, right, (((1,), (1,)), ((), ())), preferred_element_type=jnp.float32
        )

    full = (
        dot(high, weight_high_ref[0]) + dot(high, weight_low_ref[0]) + dot(low, weight_high_ref[0])
    )
    slot_of_row = lax.broadcasted_iota(jnp.int32, (slots, columns), 0)
    column = lax.broadcasted_iota(jnp.int32, (slots, columns), 1)
    first = slot_of_row * columns_per_slot
    own = (column >= first) & (column < first + columns_per_slot)
    picked = jnp.where(own[None], full.reshape(orders, slots, columns), 0.0)
    out_ref[0] = jnp.sum(picked, axis=1)


def contract_table(high, low, weight_high, weight_low, columns_per_slot):
    _, half, slots, lats = high.shape
    columns = weight_high.shape[1]
    tile = 40
    table_spec = pl.BlockSpec((1, tile, slots, lats), lambda p, i: (p, i, 0, 0))
    weight_spec = pl.BlockSpec((1, columns, lats), lambda p, i: (p, 0, 0))
    return pl.pallas_call(
        lambda *refs: contract_kernel(columns_per_slot, *refs),
        grid=(2, half // tile),
        in_specs=[table_spec, table_spec, weight_spec, weight_spec],
        out_specs=pl.BlockSpec((1, tile, columns), lambda p, i: (p, i, 0)),
        out_shape=jax.ShapeDtypeStruct((2, half, columns), jnp.float32),
        cost_estimate=pl.CostEstimate(
            flops=12 * half * slots * lats * columns,
            bytes_accessed=8 * half * slots * lats,
            transcendentals=0,
        ),
        name="legendre_contract",
    )(high, low, weight_high, weight_low)


def split_pair(values):
    high = lax.reduce_precision(values, 8, 7)
    return high.astype(jnp.bfloat16), (values - high).astype(jnp.bfloat16)


def shards(tracer, wind_east, wind_north, keep_m, slot_wave):
    groups = lax.axis_size("lev") * lax.axis_size("fld")
    lat_parts = lax.axis_size("lat")
    levels, lat_rows, _ = tracer.shape
    own_levels = levels // groups
    slots_lat = slot_wave.shape[0] // lat_parts
    slots_own = -(-slots_lat // groups)
    first_row = lax.axis_index("lat") * lat_rows

    waves = jnp.pad(
        slot_wave.reshape(lat_parts, slots_lat),
        ((0, 0), (0, groups * slots_own - slots_lat)),
        constant_values=M,
    ).reshape(-1)
    place = lax.axis_index(("lat",) + GROUP) * slots_own
    my_waves = lax.dynamic_slice_in_dim(waves, place, slots_own)

    half_lat = NLAT // 2
    lat_padded = round_up(half_lat, 128)
    slots_padded = round_up(slots_own, slot_tile)
    padded_waves = jnp.pad(my_waves, (0, slots_padded - slots_own))
    table_high, table_low = legendre_table(
        *legendre_setup(padded_waves, M, NLAT, half_lat, lat_padded)
    )

    advected = advect(tracer, wind_east, wind_north, first_row, NLAT)
    advected = lax.all_to_all(advected, GROUP, split_axis=0, concat_axis=2, tiled=True)
    fourier = jnp.einsum(
        "sck,ijk->scij", fourier_table(waves, NLON), advected, precision=lax.Precision.HIGH
    )
    kept_mask = (waves[:, None] < keep_m[None, :]).astype(jnp.float32)
    fourier = fourier * kept_mask[:, None, None, :]
    fourier = fourier.reshape(lat_parts * groups, slots_own * 2 * own_levels, lat_rows)
    spectral_in = lax.all_to_all(
        fourier, ("lat",) + GROUP, split_axis=0, concat_axis=0, tiled=True
    )
    spectral_in = spectral_in.reshape(lat_parts, groups, slots_own, 2, own_levels, lat_rows)
    columns_per_slot = levels * 2
    used = slots_own * columns_per_slot
    weighted = spectral_in.transpose(2, 1, 4, 3, 0, 5).reshape(used, NLAT)
    sines = jnp.sin(math.pi / NLAT * (jnp.arange(NLAT, dtype=jnp.float32) + 0.5))
    weighted = weighted * (sines * math.sqrt(2.0 / NLAT))[None, :]
    north = weighted[:, :half_lat]
    south = jnp.flip(weighted[:, half_lat:], axis=1)
    folded = jnp.pad(
        jnp.stack([north + south, north - south]),
        ((0, 0), (0, round_up(used, 128) - used), (0, lat_padded - half_lat)),
    )
    summed = contract_table(table_high, table_low, *split_pair(folded), columns_per_slot)
    result = summed.transpose(2, 1, 0).reshape(-1, M)[:used]
    inside = jnp.arange(M, dtype=jnp.int32)[None, :] < M - my_waves[:, None]
    result = jnp.where(
        inside[:, None, None, :], result.reshape(slots_own, levels, 2, M), 0.0
    ).transpose(1, 0, 2, 3)
    result = lax.all_to_all(
        result.reshape(groups, own_levels * slots_own * 2, M),
        GROUP,
        split_axis=0,
        concat_axis=0,
        tiled=True,
    )
    result = result.reshape(groups, own_levels, slots_own, 2, M).transpose(1, 0, 2, 3, 4)
    return result.reshape(own_levels, groups * slots_own, 2, M)[:, :slots_lat]


def solution(mesh):
    return jax.shard_map(
        shards,
        mesh=mesh,
        in_specs=(
            P("member", "lat", ("lev", "fld")),
            P("member", "lat", ("lev", "fld")),
            P("member", "lat", ("lev", "fld")),
            P("lat"),
            P(),
        ),
        out_specs=P(("member", "lev", "fld"), "lat", None, None),
        check_vma=False,
    )
```

```python
import math

import jax
import jax.numpy as jnp
from jax import lax
from jax.experimental import pallas as pl
from jax.experimental.pallas import tpu as pltpu
from jax.sharding import PartitionSpec as P

M = 400
NLAT = 800
NLON = 1600

block_rows = 16
slot_tile = 16
GROUP = ("lev", "fld")


def round_up(value, multiple):
    return -(-value // multiple) * multiple


def edges(block, axis, dim):
    count = lax.axis_size(axis)
    forward = [(i, (i + 1) % count) for i in range(count)]
    backward = [(target, source) for source, target in forward]
    low = lax.ppermute(
        lax.slice_in_dim(block, block.shape[dim] - 1, None, axis=dim), axis, forward
    )
    high = lax.ppermute(lax.slice_in_dim(block, 0, 1, axis=dim), axis, backward)
    return low, high


def fourier_table(row_waves, lon_count, quarter_turns):
    grid_index = jnp.arange(lon_count, dtype=jnp.int32)
    shift = quarter_turns * (lon_count // 4)
    phase_index = (row_waves[:, None] * grid_index[None, :] + shift[:, None]) % lon_count
    angles = 2.0 * math.pi / lon_count * phase_index.astype(jnp.float32)
    return jnp.cos(angles) * (1.0 / math.sqrt(lon_count))


def advect_kernel(
    tracer_ref, east_wind_ref, north_wind_ref, west_ref, east_ref, above_ref, below_ref, out_ref, pad_ref
):
    _, rows, columns = out_ref.shape
    tall, wide = pad_ref.shape
    centre = tracer_ref[0].astype(jnp.float32)
    pad_ref[:rows, :columns] = centre
    pad_ref[:rows, columns : columns + 1] = east_ref[0].astype(jnp.float32)
    pad_ref[:rows, wide - 1 : wide] = west_ref[0].astype(jnp.float32)
    pad_ref[rows : rows + 1, :columns] = below_ref[0]
    pad_ref[tall - 1 : tall, :columns] = above_ref[0]
    full = pad_ref[...]
    east_diff = (pltpu.roll(full, wide - 1, 1) - pltpu.roll(full, 1, 1))[:rows, :columns]
    north_diff = (pltpu.roll(full, tall - 1, 0) - pltpu.roll(full, 1, 0))[:rows, :columns]
    out_ref[0] = (
        centre
        - 0.5 * east_wind_ref[0].astype(jnp.float32) * east_diff
        - 0.5 * north_wind_ref[0].astype(jnp.float32) * north_diff
    )


def advect(tracer, east_wind, north_wind, first_row, lat_total):
    west, east = edges(tracer, GROUP, 2)
    above, below = edges(tracer, "lat", 1)
    levels, rows, columns = tracer.shape
    has_above = (first_row > 0).astype(jnp.float32)
    has_below = (first_row + rows < lat_total).astype(jnp.float32)
    above = above.astype(jnp.float32) * has_above
    below = below.astype(jnp.float32) * has_below
    block = pl.BlockSpec((1, rows, columns), lambda i: (i, 0, 0))
    column = pl.BlockSpec((1, rows, 1), lambda i: (i, 0, 0))
    line = pl.BlockSpec((1, 1, columns), lambda i: (i, 0, 0))
    size = levels * rows * columns
    return pl.pallas_call(
        advect_kernel,
        grid=(levels,),
        in_specs=[block, block, block, column, column, line, line],
        out_specs=block,
        out_shape=jax.ShapeDtypeStruct(tracer.shape, jnp.float32),
        scratch_shapes=[pltpu.VMEM((round_up(rows + 2, 8), round_up(columns + 2, 128)), jnp.float32)],
        cost_estimate=pl.CostEstimate(
            flops=10 * size, bytes_accessed=10 * size, transcendentals=0
        ),
        name="advect",
    )(tracer, east_wind, north_wind, west, east, above, below)


def split_high_low(values):
    high = values.astype(jnp.bfloat16)
    return high, (values - high.astype(jnp.float32)).astype(jnp.bfloat16)


def product(left, right):
    return lax.dot_general(
        left, right, (((1,), (1,)), ((), ())), preferred_element_type=jnp.float32
    )


def fourier_kernel(rows_own, table_ref, field_ref, wave_ref, keep_ref, out_ref, total_ref):
    step = pl.program_id(0)
    _, levels, lat_rows, _ = field_ref.shape
    targets = out_ref.shape[0]
    rows_padded = table_ref.shape[1] // targets
    table_high, table_low = split_high_low(table_ref[0])
    for level in range(levels):
        field_high, field_low = split_high_low(field_ref[0, level])
        term = (
            product(table_high, field_high)
            + product(table_high, field_low)
            + product(table_low, field_high)
        )

        @pl.when(step == 0)
        def _():
            total_ref[level] = term

        @pl.when(step > 0)
        def _():
            total_ref[level] += term

    @pl.when(step == pl.num_programs(0) - 1)
    def _():
        kept = wave_ref[...] < keep_ref[...]
        for level in range(levels):
            masked = jnp.where(kept, total_ref[level], 0.0)
            for target in range(targets):
                first = target * rows_padded
                out_ref[target, level * rows_own : (level + 1) * rows_own] = masked[
                    first : first + rows_own
                ]


def fourier_transform(table, field, row_waves, keep_m, targets, rows_own):
    chunks, levels, lat_rows, lons = field.shape
    rows = row_waves.shape[0]
    return pl.pallas_call(
        lambda *refs: fourier_kernel(rows_own, *refs),
        grid=(chunks,),
        in_specs=[
            pl.BlockSpec((1, rows, lons), lambda i: (i, 0, 0)),
            pl.BlockSpec((1, levels, lat_rows, lons), lambda i: (i, 0, 0, 0)),
            pl.BlockSpec((rows, 1), lambda i: (0, 0)),
            pl.BlockSpec((1, lat_rows), lambda i: (0, 0)),
        ],
        out_specs=pl.BlockSpec((targets, levels * rows_own, lat_rows), lambda i: (0, 0, 0)),
        out_shape=jax.ShapeDtypeStruct((targets, levels * rows_own, lat_rows), jnp.float32),
        scratch_shapes=[pltpu.VMEM((levels, rows, lat_rows), jnp.float32)],
        cost_estimate=pl.CostEstimate(
            flops=6 * rows * chunks * levels * lat_rows * lons,
            bytes_accessed=4 * rows * chunks * lons,
            transcendentals=0,
        ),
        name="fourier_transform",
    )(table, field, row_waves[:, None], keep_m[None, :])


def legendre_setup(wave_ids, trunc_count, lat_total, lat_used, lat_padded):
    degree = jnp.minimum(wave_ids, trunc_count - 1).astype(jnp.float32)
    counter = jnp.arange(1, trunc_count, dtype=jnp.float32)
    log_terms = jnp.log1p(0.5 / counter)
    log_norm = jnp.sum(
        jnp.where(counter[None, :] <= degree[:, None], log_terms[None, :], 0.0), axis=1
    )
    rows = jnp.minimum(jnp.arange(lat_padded), lat_used - 1)
    colatitude = math.pi / lat_total * (rows.astype(jnp.float32) + 0.5)
    start_log = 0.5 * (log_norm[:, None] - math.log(2.0)) + degree[:, None] * jnp.log(
        jnp.sin(colatitude)
    )
    orders = jnp.arange(1, trunc_count + 1, dtype=jnp.float32)
    total = degree[:, None] + orders
    square = degree[:, None] * degree[:, None]
    growth = jnp.sqrt((4.0 * total * total - 1.0) / (total * total - square))
    lower = total - 1.0
    damping = jnp.sqrt(
        (lower * lower - square) / jnp.maximum(4.0 * lower * lower - 1.0, 1.0)
    )

    def blocked(values):
        return values.reshape(values.shape[0], -1, block_rows).transpose(1, 0, 2)

    return blocked(growth), blocked(damping), jnp.cos(colatitude)[None, :], start_log


def table_kernel(growth_ref, damping_ref, cosine_ref, start_ref, high_ref, low_ref):
    cosine = cosine_ref[...]
    shape = start_ref.shape

    def advance(index, carry):
        before, current, log_scale = carry
        scale = jnp.exp(log_scale)
        growth = growth_ref[index]
        damping = damping_ref[index]
        for offset in range(block_rows):
            row = current * scale
            high = row.astype(jnp.bfloat16)
            low = (row - high.astype(jnp.float32)).astype(jnp.bfloat16)
            place = index * (block_rows // 2) + offset // 2
            high_ref[offset % 2, place] = high
            low_ref[offset % 2, place] = low
            advanced = growth[:, offset : offset + 1] * (
                cosine * current - damping[:, offset : offset + 1] * before
            )
            before, current = current, advanced
        biggest = jnp.maximum(jnp.abs(before), jnp.abs(current))
        return before / biggest, current / biggest, log_scale + jnp.log(biggest)

    lax.fori_loop(
        0,
        growth_ref.shape[0],
        advance,
        (jnp.zeros(shape, jnp.float32), jnp.ones(shape, jnp.float32), start_ref[...]),
    )


def legendre_table(growth, damping, cosine, start_log):
    blocks, slots, _ = growth.shape
    lats = cosine.shape[1]
    half = blocks * block_rows // 2
    out = jax.ShapeDtypeStruct((2, half, slots, lats), jnp.bfloat16)
    coef_spec = pl.BlockSpec((blocks, slot_tile, block_rows), lambda i: (0, i, 0))
    out_spec = pl.BlockSpec((2, half, slot_tile, lats), lambda i: (0, 0, i, 0))
    size = 2 * half * slots * lats
    return pl.pallas_call(
        table_kernel,
        grid=(slots // slot_tile,),
        in_specs=[
            coef_spec,
            coef_spec,
            pl.BlockSpec((1, lats), lambda i: (0, 0)),
            pl.BlockSpec((slot_tile, lats), lambda i: (i, 0)),
        ],
        out_specs=[out_spec, out_spec],
        out_shape=[out, out],
        cost_estimate=pl.CostEstimate(
            flops=10 * size, bytes_accessed=4 * size, transcendentals=size // 4
        ),
        name="legendre_table",
    )(growth, damping, cosine, start_log)


def contract_kernel(
    high_ref, low_ref, weight_high_ref, weight_low_ref, own_ref, limit_ref, out_ref, sums_ref
):
    step = pl.program_id(0)
    _, orders, slots, lats = high_ref.shape
    lane_tiles, _, lanes = sums_ref.shape
    levels, rows_own, order_total = out_ref.shape
    own = own_ref[...] > 0.0
    for parity in range(2):
        high = high_ref[parity].reshape(orders * slots, lats)
        low = low_ref[parity].reshape(orders * slots, lats)
        full = (
            product(high, weight_high_ref[parity])
            + product(high, weight_low_ref[parity])
            + product(low, weight_high_ref[parity])
        )
        picked = jnp.where(own[None], full.reshape(orders, slots, lane_tiles * lanes), 0.0)
        summed = jnp.sum(picked, axis=1)
        for tile in range(lane_tiles):
            sums_ref[tile, pl.ds(step * 2 * orders + parity, orders, stride=2), :] = summed[
                :, tile * lanes : (tile + 1) * lanes
            ]

    @pl.when(step == pl.num_programs(0) - 1)
    def _():
        turned = jnp.concatenate([sums_ref[tile].T for tile in range(lane_tiles)], axis=0)
        turned = turned[:, :order_total]
        order = lax.broadcasted_iota(jnp.int32, turned.shape, 1)
        turned = jnp.where(order < limit_ref[...], turned, 0.0)
        for level in range(levels):
            out_ref[level] = turned[level * rows_own : (level + 1) * rows_own]


def contract_table(high, low, weight_high, weight_low, own, limit, levels, rows_own):
    _, half, slots, lats = high.shape
    columns = weight_high.shape[1]
    tile = 20
    table_spec = pl.BlockSpec((2, tile, slots, lats), lambda i: (0, i, 0, 0))
    weight_spec = pl.BlockSpec((2, columns, lats), lambda i: (0, 0, 0))
    return pl.pallas_call(
        contract_kernel,
        grid=(half // tile,),
        in_specs=[
            table_spec,
            table_spec,
            weight_spec,
            weight_spec,
            pl.BlockSpec((slots, columns), lambda i: (0, 0)),
            pl.BlockSpec((columns, 1), lambda i: (0, 0)),
        ],
        out_specs=pl.BlockSpec((levels, rows_own, 2 * half), lambda i: (0, 0, 0)),
        out_shape=jax.ShapeDtypeStruct((levels, rows_own, 2 * half), jnp.float32),
        scratch_shapes=[pltpu.VMEM((columns // 128, round_up(2 * half, 128), 128), jnp.float32)],
        cost_estimate=pl.CostEstimate(
            flops=12 * half * slots * lats * columns,
            bytes_accessed=8 * half * slots * lats,
            transcendentals=0,
        ),
        name="legendre_contract",
    )(high, low, weight_high, weight_low, own, limit)


def split_pair(values):
    high = lax.reduce_precision(values, 8, 7)
    return high.astype(jnp.bfloat16), (values - high).astype(jnp.bfloat16)


def shards(tracer, wind_east, wind_north, keep_m, slot_wave):
    groups = lax.axis_size("lev") * lax.axis_size("fld")
    lat_parts = lax.axis_size("lat")
    levels, lat_rows, _ = tracer.shape
    own_levels = levels // groups
    slots_lat = slot_wave.shape[0] // lat_parts
    slots_own = -(-slots_lat // groups)
    first_row = lax.axis_index("lat") * lat_rows

    waves = jnp.pad(
        slot_wave.reshape(lat_parts, slots_lat),
        ((0, 0), (0, groups * slots_own - slots_lat)),
        constant_values=M,
    ).reshape(-1)
    place = lax.axis_index(("lat",) + GROUP) * slots_own
    my_waves = lax.dynamic_slice_in_dim(waves, place, slots_own)

    half_lat = NLAT // 2
    lat_padded = round_up(half_lat, 128)
    slots_padded = round_up(slots_own, slot_tile)
    padded_waves = jnp.pad(my_waves, (0, slots_padded - slots_own))
    table_high, table_low = legendre_table(
        *legendre_setup(padded_waves, M, NLAT, half_lat, lat_padded)
    )

    targets = lat_parts * groups
    rows_own = slots_own * 2
    rows_padded = round_up(rows_own, 8)
    row_waves = jnp.pad(
        jnp.repeat(waves.reshape(targets, slots_own), 2, axis=1),
        ((0, 0), (0, rows_padded - rows_own)),
        constant_values=M,
    ).reshape(-1)
    table = fourier_table(row_waves, NLON, jnp.arange(targets * rows_padded, dtype=jnp.int32) % 2)
    table = table.reshape(-1, groups, NLON // groups).transpose(1, 0, 2)

    advected = advect(tracer, wind_east, wind_north, first_row, NLAT)
    advected = lax.all_to_all(advected, GROUP, split_axis=0, concat_axis=0, tiled=True)
    advected = advected.reshape(groups, own_levels, lat_rows, -1)
    fourier = fourier_transform(table, advected, row_waves, keep_m, targets, rows_own)
    spectral_in = lax.all_to_all(
        fourier, ("lat",) + GROUP, split_axis=0, concat_axis=0, tiled=True
    )
    used = levels * rows_own
    weighted = spectral_in.reshape(lat_parts, used, lat_rows).transpose(1, 0, 2)
    weighted = weighted.reshape(used, NLAT)
    sines = jnp.sin(math.pi / NLAT * (jnp.arange(NLAT, dtype=jnp.float32) + 0.5))
    weighted = weighted * (sines * math.sqrt(2.0 / NLAT))[None, :]
    north = weighted[:, :half_lat]
    south = jnp.flip(weighted[:, half_lat:], axis=1)
    columns = round_up(used, 128)
    folded = jnp.pad(
        jnp.stack([north + south, north - south]),
        ((0, 0), (0, columns - used), (0, lat_padded - half_lat)),
    )
    slot_of_column = jnp.arange(columns, dtype=jnp.int32) % rows_own // 2
    own = (jnp.arange(slots_padded, dtype=jnp.int32)[:, None] == slot_of_column[None, :]).astype(
        jnp.float32
    )
    limit = (M - my_waves)[slot_of_column][:, None]
    result = contract_table(
        table_high, table_low, *split_pair(folded), own, limit, levels, rows_own
    )
    result = lax.all_to_all(result, GROUP, split_axis=0, concat_axis=0, tiled=True)
    result = result.reshape(groups, own_levels, slots_own, 2, M).transpose(1, 0, 2, 3, 4)
    return result.reshape(own_levels, groups * slots_own, 2, M)[:, :slots_lat]


def solution(mesh):
    return jax.shard_map(
        shards,
        mesh=mesh,
        in_specs=(
            P("member", "lat", ("lev", "fld")),
            P("member", "lat", ("lev", "fld")),
            P("member", "lat", ("lev", "fld")),
            P("lat"),
            P(),
        ),
        out_specs=P(("member", "lev", "fld"), "lat", None, None),
        check_vma=False,
    )
```

```python
import math

import jax
import jax.numpy as jnp
from jax import lax
from jax.experimental import pallas as pl
from jax.experimental.pallas import tpu as pltpu
from jax.sharding import PartitionSpec as P

M = 400
NLAT = 800
NLON = 1600

block_rows = 16
slot_tile = 8
order_tile = 80
LANES = 128
GROUP = ("lev", "fld")


def round_up(value, multiple):
    return -(-value // multiple) * multiple


def edges(block, axis, dim):
    count = lax.axis_size(axis)
    forward = [(i, (i + 1) % count) for i in range(count)]
    backward = [(target, source) for source, target in forward]
    low = lax.ppermute(
        lax.slice_in_dim(block, block.shape[dim] - 1, None, axis=dim), axis, forward
    )
    high = lax.ppermute(lax.slice_in_dim(block, 0, 1, axis=dim), axis, backward)
    return low, high


def fourier_factors(row_waves, quarter_turns, offsets, lon_count):
    step = 2.0 * math.pi / lon_count
    lane = row_waves[:, None] * jnp.arange(LANES, dtype=jnp.int32)[None, :] % lon_count
    lane = step * lane.astype(jnp.float32)
    shift = quarter_turns * (lon_count // 4)
    base = (offsets[:, None] * row_waves[None, :] + shift[None, :]) % lon_count
    base = step * base.astype(jnp.float32)
    factor = 1.0 / math.sqrt(lon_count)
    return (jnp.cos(base) * factor).T, (jnp.sin(base) * factor).T, jnp.cos(lane), jnp.sin(lane)


def wave_table_kernel(base_cos_ref, base_sin_ref, lane_cos_ref, lane_sin_ref, high_ref, low_ref):
    chunks, _, wide = high_ref.shape
    tiles = wide // LANES
    lane_cos = lane_cos_ref[...]
    lane_sin = lane_sin_ref[...]
    for chunk in range(chunks):
        for tile in range(tiles):
            k = chunk * tiles + tile
            values = (
                base_cos_ref[:, k : k + 1] * lane_cos - base_sin_ref[:, k : k + 1] * lane_sin
            )
            high, low = split_high_low(values)
            high_ref[chunk, :, tile * LANES : (tile + 1) * LANES] = high
            low_ref[chunk, :, tile * LANES : (tile + 1) * LANES] = low


def fourier_table(row_waves, quarter_turns, chunks, lons, lon_count):
    tiles = -(-lons // LANES)
    offsets = (
        jnp.arange(chunks, dtype=jnp.int32)[:, None] * lons
        + jnp.arange(tiles, dtype=jnp.int32)[None, :] * LANES
    ).reshape(-1)
    factors = fourier_factors(row_waves, quarter_turns, offsets, lon_count)
    rows = row_waves.shape[0]
    tall = math.gcd(rows, 128)
    out = jax.ShapeDtypeStruct((chunks, rows, tiles * LANES), jnp.bfloat16)
    out_spec = pl.BlockSpec((chunks, tall, tiles * LANES), lambda i: (0, i, 0))
    size = chunks * rows * tiles * LANES
    return pl.pallas_call(
        wave_table_kernel,
        grid=(rows // tall,),
        in_specs=[pl.BlockSpec((tall, f.shape[1]), lambda i: (i, 0)) for f in factors],
        out_specs=[out_spec, out_spec],
        out_shape=[out, out],
        cost_estimate=pl.CostEstimate(flops=8 * size, bytes_accessed=4 * size, transcendentals=0),
        name="fourier_table",
    )(*factors)


def advect_kernel(
    tracer_ref, east_wind_ref, north_wind_ref, west_ref, east_ref, above_ref, below_ref, out_ref, pad_ref
):
    _, rows, columns = out_ref.shape
    tall, wide = pad_ref.shape
    centre = tracer_ref[0].astype(jnp.float32)
    pad_ref[:rows, :columns] = centre
    pad_ref[:rows, columns : columns + 1] = east_ref[0].astype(jnp.float32)
    pad_ref[:rows, wide - 1 : wide] = west_ref[0].astype(jnp.float32)
    pad_ref[rows : rows + 1, :columns] = below_ref[0]
    pad_ref[tall - 1 : tall, :columns] = above_ref[0]
    full = pad_ref[...]
    east_diff = (pltpu.roll(full, wide - 1, 1) - pltpu.roll(full, 1, 1))[:rows, :columns]
    north_diff = (pltpu.roll(full, tall - 1, 0) - pltpu.roll(full, 1, 0))[:rows, :columns]
    out_ref[0] = (
        centre
        - 0.5 * east_wind_ref[0].astype(jnp.float32) * east_diff
        - 0.5 * north_wind_ref[0].astype(jnp.float32) * north_diff
    )


def advect(tracer, east_wind, north_wind, first_row, lat_total):
    west, east = edges(tracer, GROUP, 2)
    above, below = edges(tracer, "lat", 1)
    levels, rows, columns = tracer.shape
    has_above = (first_row > 0).astype(jnp.float32)
    has_below = (first_row + rows < lat_total).astype(jnp.float32)
    above = above.astype(jnp.float32) * has_above
    below = below.astype(jnp.float32) * has_below
    block = pl.BlockSpec((1, rows, columns), lambda i: (i, 0, 0))
    column = pl.BlockSpec((1, rows, 1), lambda i: (i, 0, 0))
    line = pl.BlockSpec((1, 1, columns), lambda i: (i, 0, 0))
    size = levels * rows * columns
    return pl.pallas_call(
        advect_kernel,
        grid=(levels,),
        in_specs=[block, block, block, column, column, line, line],
        out_specs=block,
        out_shape=jax.ShapeDtypeStruct(tracer.shape, jnp.float32),
        scratch_shapes=[pltpu.VMEM((round_up(rows + 2, 8), round_up(columns + 2, 128)), jnp.float32)],
        cost_estimate=pl.CostEstimate(
            flops=10 * size, bytes_accessed=10 * size, transcendentals=0
        ),
        name="advect",
    )(tracer, east_wind, north_wind, west, east, above, below)


def split_high_low(values):
    high = values.astype(jnp.bfloat16)
    return high, (values - high.astype(jnp.float32)).astype(jnp.bfloat16)


def product(left, right):
    return lax.dot_general(
        left, right, (((1,), (1,)), ((), ())), preferred_element_type=jnp.float32
    )


def fourier_kernel(
    rows_own, table_high_ref, table_low_ref, field_ref, wave_ref, keep_ref, out_ref, total_ref
):
    step = pl.program_id(0)
    _, levels, lat_rows, lons = field_ref.shape
    targets = out_ref.shape[0]
    rows_padded = table_high_ref.shape[1] // targets
    table_high = table_high_ref[0][:, :lons]
    table_low = table_low_ref[0][:, :lons]
    for level in range(levels):
        field_high, field_low = split_high_low(field_ref[0, level])
        term = (
            product(table_high, field_high)
            + product(table_high, field_low)
            + product(table_low, field_high)
        )

        @pl.when(step == 0)
        def _():
            total_ref[level] = term

        @pl.when(step > 0)
        def _():
            total_ref[level] += term

    @pl.when(step == pl.num_programs(0) - 1)
    def _():
        kept = wave_ref[...] < keep_ref[...]
        for level in range(levels):
            masked = jnp.where(kept, total_ref[level], 0.0)
            for target in range(targets):
                first = target * rows_padded
                out_ref[target, level * rows_own : (level + 1) * rows_own] = masked[
                    first : first + rows_own
                ]


def fourier_transform(table, field, row_waves, keep_m, targets, rows_own):
    chunks, levels, lat_rows, lons = field.shape
    rows = row_waves.shape[0]
    table_spec = pl.BlockSpec((1, rows, table[0].shape[2]), lambda i: (i, 0, 0))
    return pl.pallas_call(
        lambda *refs: fourier_kernel(rows_own, *refs),
        grid=(chunks,),
        in_specs=[
            table_spec,
            table_spec,
            pl.BlockSpec((1, levels, lat_rows, lons), lambda i: (i, 0, 0, 0)),
            pl.BlockSpec((rows, 1), lambda i: (0, 0)),
            pl.BlockSpec((1, lat_rows), lambda i: (0, 0)),
        ],
        out_specs=pl.BlockSpec((targets, levels * rows_own, lat_rows), lambda i: (0, 0, 0)),
        out_shape=jax.ShapeDtypeStruct((targets, levels * rows_own, lat_rows), jnp.float32),
        scratch_shapes=[pltpu.VMEM((levels, rows, lat_rows), jnp.float32)],
        cost_estimate=pl.CostEstimate(
            flops=6 * rows * chunks * levels * lat_rows * lons,
            bytes_accessed=4 * rows * chunks * lons,
            transcendentals=0,
        ),
        name="fourier_transform",
    )(*table, field, row_waves[:, None], keep_m[None, :])


def legendre_setup(wave_ids, trunc_count, lat_total, lat_used, lat_padded):
    degree = jnp.minimum(wave_ids, trunc_count - 1).astype(jnp.float32)
    counter = jnp.arange(1, trunc_count, dtype=jnp.float32)
    log_terms = jnp.log1p(0.5 / counter)
    log_norm = jnp.sum(
        jnp.where(counter[None, :] <= degree[:, None], log_terms[None, :], 0.0), axis=1
    )
    rows = jnp.minimum(jnp.arange(lat_padded), lat_used - 1)
    colatitude = math.pi / lat_total * (rows.astype(jnp.float32) + 0.5)
    start_log = 0.5 * (log_norm[:, None] - math.log(2.0)) + degree[:, None] * jnp.log(
        jnp.sin(colatitude)
    )
    orders = jnp.arange(1, trunc_count + 1, dtype=jnp.float32)
    total = degree[:, None] + orders
    square = degree[:, None] * degree[:, None]
    growth = jnp.sqrt((4.0 * total * total - 1.0) / (total * total - square))
    lower = total - 1.0
    damping = jnp.sqrt(
        (lower * lower - square) / jnp.maximum(4.0 * lower * lower - 1.0, 1.0)
    )

    def blocked(values):
        return values.reshape(values.shape[0], -1, block_rows).transpose(1, 0, 2)

    return blocked(growth), blocked(damping), jnp.cos(colatitude)[None, :], start_log


def table_kernel(
    blocks_ref, growth_ref, damping_ref, cosine_ref, start_ref, high_ref, low_ref
):
    shape = start_ref.shape
    cosine = jnp.broadcast_to(cosine_ref[...], shape)
    slots = shape[0]
    wide = block_rows // 2 * slots

    def advance(index, carry):
        before, current, log_scale = carry
        scale = jnp.exp(log_scale)
        growth = growth_ref[index]
        damping = damping_ref[index]
        rows = []
        for offset in range(block_rows):
            rows.append(current * scale)
            advanced = growth[:, offset : offset + 1] * (
                cosine * current - damping[:, offset : offset + 1] * before
            )
            before, current = current, advanced
            if offset % 4 == 3:
                for parity in range(2):
                    pair = jnp.concatenate([rows[offset - 3 + parity], rows[offset - 1 + parity]])
                    high, low = split_high_low(pair)
                    first = pl.multiple_of(index * wide + offset // 4 * 2 * slots, 2 * slots)
                    high_ref[parity, 0, pl.ds(first, 2 * slots)] = high
                    low_ref[parity, 0, pl.ds(first, 2 * slots)] = low
        biggest = jnp.maximum(jnp.abs(before), jnp.abs(current))
        return before / biggest, current / biggest, log_scale + jnp.log(biggest)

    lax.fori_loop(
        0,
        blocks_ref[pl.program_id(0)] * (order_tile // block_rows),
        advance,
        (jnp.zeros(shape, jnp.float32), jnp.ones(shape, jnp.float32), start_ref[...]),
    )


def legendre_table(blocks_used, growth, damping, cosine, start_log):
    blocks, slots, _ = growth.shape
    lats = cosine.shape[1]
    rows = blocks * block_rows // 2 * slot_tile
    tiles = slots // slot_tile
    out = jax.ShapeDtypeStruct((2, tiles, rows, lats), jnp.bfloat16)
    coef_spec = pl.BlockSpec((blocks, slot_tile, block_rows), lambda i, used: (0, i, 0))
    out_spec = pl.BlockSpec((2, 1, rows, lats), lambda i, used: (0, i, 0, 0))
    size = 2 * tiles * rows * lats
    return pl.pallas_call(
        table_kernel,
        grid_spec=pltpu.PrefetchScalarGridSpec(
            num_scalar_prefetch=1,
            grid=(tiles,),
            in_specs=[
                coef_spec,
                coef_spec,
                pl.BlockSpec((1, lats), lambda i, used: (0, 0)),
                pl.BlockSpec((slot_tile, lats), lambda i, used: (i, 0)),
            ],
            out_specs=[out_spec, out_spec],
        ),
        out_shape=[out, out],
        cost_estimate=pl.CostEstimate(
            flops=10 * size, bytes_accessed=4 * size, transcendentals=size // 4
        ),
        name="legendre_table",
    )(blocks_used, growth, damping, cosine, start_log)


def contract_kernel(
    blocks_ref,
    high_ref,
    low_ref,
    weight_high_ref,
    weight_low_ref,
    own_ref,
    limit_ref,
    out_ref,
    sums_ref,
):
    tile = pl.program_id(0)
    step = pl.program_id(1)
    rows = high_ref.shape[2]
    slots = own_ref.shape[0]
    orders = rows // slots
    lane_tiles, _, lanes = sums_ref.shape
    levels, rows_own, order_total = out_ref.shape

    @pl.when((tile == 0) & (step == 0))
    def _():
        sums_ref[...] = jnp.zeros_like(sums_ref)

    @pl.when(step < blocks_ref[tile])
    def _():
        own = own_ref[...] > 0.0
        for parity in range(2):
            full = (
                product(high_ref[parity, 0], weight_high_ref[parity])
                + product(high_ref[parity, 0], weight_low_ref[parity])
                + product(low_ref[parity, 0], weight_high_ref[parity])
            )
            picked = jnp.where(own[None], full.reshape(orders, slots, lane_tiles * lanes), 0.0)
            summed = jnp.sum(picked, axis=1)
            for k in range(lane_tiles):
                place = pl.ds(step * 2 * orders + parity, orders, stride=2)
                sums_ref[k, place, :] += summed[:, k * lanes : (k + 1) * lanes]

    @pl.when((tile == pl.num_programs(0) - 1) & (step == pl.num_programs(1) - 1))
    def _():
        turned = jnp.concatenate([sums_ref[k].T for k in range(lane_tiles)], axis=0)
        turned = turned[:, :order_total]
        order = lax.broadcasted_iota(jnp.int32, turned.shape, 1)
        turned = jnp.where(order < limit_ref[...], turned, 0.0)
        for level in range(levels):
            out_ref[level] = turned[level * rows_own : (level + 1) * rows_own]


def contract_table(
    blocks_used, high, low, weight_high, weight_low, own, limit, levels, rows_own
):
    _, tiles, rows, lats = high.shape
    columns = weight_high.shape[1]
    block = order_tile // 2 * slot_tile
    order_total = 2 * rows // slot_tile

    def table_map(i, j, used):
        return (0, i, jnp.maximum(jnp.minimum(j, used[i] - 1), 0), 0)

    table_spec = pl.BlockSpec((2, 1, block, lats), table_map)
    weight_spec = pl.BlockSpec((2, columns, lats), lambda i, j, used: (0, 0, 0))
    return pl.pallas_call(
        contract_kernel,
        grid_spec=pltpu.PrefetchScalarGridSpec(
            num_scalar_prefetch=1,
            grid=(tiles, rows // block),
            in_specs=[
                table_spec,
                table_spec,
                weight_spec,
                weight_spec,
                pl.BlockSpec((slot_tile, columns), lambda i, j, used: (i, 0)),
                pl.BlockSpec((columns, 1), lambda i, j, used: (0, 0)),
            ],
            out_specs=pl.BlockSpec((levels, rows_own, order_total), lambda i, j, used: (0, 0, 0)),
            scratch_shapes=[
                pltpu.VMEM((columns // LANES, round_up(order_total, LANES), LANES), jnp.float32)
            ],
        ),
        out_shape=jax.ShapeDtypeStruct((levels, rows_own, order_total), jnp.float32),
        cost_estimate=pl.CostEstimate(
            flops=12 * tiles * rows * lats * columns,
            bytes_accessed=8 * tiles * rows * lats,
            transcendentals=0,
        ),
        name="legendre_contract",
    )(blocks_used, high, low, weight_high, weight_low, own, limit)


def split_pair(values):
    high = lax.reduce_precision(values, 8, 7)
    return high.astype(jnp.bfloat16), (values - high).astype(jnp.bfloat16)


def shards(tracer, wind_east, wind_north, keep_m, slot_wave):
    groups = lax.axis_size("lev") * lax.axis_size("fld")
    lat_parts = lax.axis_size("lat")
    levels, lat_rows, _ = tracer.shape
    own_levels = levels // groups
    slots_lat = slot_wave.shape[0] // lat_parts
    slots_own = -(-slots_lat // groups)
    first_row = lax.axis_index("lat") * lat_rows

    waves = jnp.pad(
        slot_wave.reshape(lat_parts, slots_lat),
        ((0, 0), (0, groups * slots_own - slots_lat)),
        constant_values=M,
    ).reshape(-1)
    place = lax.axis_index(("lat",) + GROUP) * slots_own
    my_waves = lax.dynamic_slice_in_dim(waves, place, slots_own)

    half_lat = NLAT // 2
    lat_padded = round_up(half_lat, 128)
    slots_padded = round_up(slots_own, slot_tile)
    index = jnp.arange(slots_own, dtype=jnp.int32)
    larger = (my_waves[None, :] > my_waves[:, None]) | (
        (my_waves[None, :] == my_waves[:, None]) & (index[None, :] < index[:, None])
    )
    row_of_slot = jnp.sum(larger.astype(jnp.int32), axis=1) + (slots_padded - slots_own)
    row_ids = jnp.arange(slots_padded, dtype=jnp.int32)
    placed = row_of_slot[None, :] == row_ids[:, None]
    padded_waves = M - jnp.sum(jnp.where(placed, M - my_waves[None, :], 0), axis=1)
    longest = jnp.max((M - padded_waves).reshape(-1, slot_tile), axis=1)
    blocks_used = jnp.maximum(-(-longest // order_tile), 0)
    table_high, table_low = legendre_table(
        blocks_used, *legendre_setup(padded_waves, M, NLAT, half_lat, lat_padded)
    )

    targets = lat_parts * groups
    rows_own = slots_own * 2
    rows_padded = round_up(rows_own, 8)
    row_waves = jnp.pad(
        jnp.repeat(waves.reshape(targets, slots_own), 2, axis=1),
        ((0, 0), (0, rows_padded - rows_own)),
        constant_values=M,
    ).reshape(-1)
    turns = jnp.arange(targets * rows_padded, dtype=jnp.int32) % 2
    table = fourier_table(row_waves, turns, groups, NLON // groups, NLON)

    advected = advect(tracer, wind_east, wind_north, first_row, NLAT)
    advected = lax.all_to_all(advected, GROUP, split_axis=0, concat_axis=0, tiled=True)
    advected = advected.reshape(groups, own_levels, lat_rows, -1)
    fourier = fourier_transform(table, advected, row_waves, keep_m, targets, rows_own)
    spectral_in = lax.all_to_all(
        fourier, ("lat",) + GROUP, split_axis=0, concat_axis=0, tiled=True
    )
    used = levels * rows_own
    weighted = spectral_in.reshape(lat_parts, used, lat_rows).transpose(1, 0, 2)
    weighted = weighted.reshape(used, NLAT)
    sines = jnp.sin(math.pi / NLAT * (jnp.arange(NLAT, dtype=jnp.float32) + 0.5))
    weighted = weighted * (sines * math.sqrt(2.0 / NLAT))[None, :]
    north = weighted[:, :half_lat]
    south = jnp.flip(weighted[:, half_lat:], axis=1)
    columns = round_up(used, 128)
    folded = jnp.pad(
        jnp.stack([north + south, north - south]),
        ((0, 0), (0, columns - used), (0, lat_padded - half_lat)),
    )
    slot_of_column = jnp.arange(columns, dtype=jnp.int32) % rows_own // 2
    column_of_row = slot_of_column[None, :, None] == index[None, None, :]
    own = jnp.any(column_of_row & placed[:, None, :], axis=2).astype(jnp.float32)
    limit = jnp.sum(jnp.where(column_of_row[0], M - my_waves[None, :], 0), axis=1)[:, None]
    result = contract_table(
        blocks_used, table_high, table_low, *split_pair(folded), own, limit, levels, rows_own
    )
    result = lax.all_to_all(result, GROUP, split_axis=0, concat_axis=0, tiled=True)
    result = result.reshape(groups, own_levels, slots_own, 2, M).transpose(1, 0, 2, 3, 4)
    return result.reshape(own_levels, groups * slots_own, 2, M)[:, :slots_lat]


def solution(mesh):
    return jax.shard_map(
        shards,
        mesh=mesh,
        in_specs=(
            P("member", "lat", ("lev", "fld")),
            P("member", "lat", ("lev", "fld")),
            P("member", "lat", ("lev", "fld")),
            P("lat"),
            P(),
        ),
        out_specs=P(("member", "lev", "fld"), "lat", None, None),
        check_vma=False,
    )
```

```python
import math

import jax
import jax.numpy as jnp
from jax import lax
from jax.experimental import pallas as pl
from jax.experimental.pallas import tpu as pltpu
from jax.sharding import PartitionSpec as P

M = 400
NLAT = 800
NLON = 1600

block_rows = 16
slot_tile = 8
order_tile = 80
LANES = 128
GROUP = ("lev", "fld")


def round_up(value, multiple):
    return -(-value // multiple) * multiple


def edges(block, axis, dim):
    count = lax.axis_size(axis)
    forward = [(i, (i + 1) % count) for i in range(count)]
    backward = [(target, source) for source, target in forward]
    low = lax.ppermute(
        lax.slice_in_dim(block, block.shape[dim] - 1, None, axis=dim), axis, forward
    )
    high = lax.ppermute(lax.slice_in_dim(block, 0, 1, axis=dim), axis, backward)
    return low, high


def fourier_factors(row_waves, quarter_turns, offsets, lon_count):
    step = 2.0 * math.pi / lon_count
    lane = row_waves[:, None] * jnp.arange(LANES, dtype=jnp.int32)[None, :] % lon_count
    lane = step * lane.astype(jnp.float32)
    shift = quarter_turns * (lon_count // 4)
    base = (offsets[:, None] * row_waves[None, :] + shift[None, :]) % lon_count
    base = step * base.astype(jnp.float32)
    factor = 1.0 / math.sqrt(lon_count)
    return (jnp.cos(base) * factor).T, (jnp.sin(base) * factor).T, jnp.cos(lane), jnp.sin(lane)


def wave_table_kernel(base_cos_ref, base_sin_ref, lane_cos_ref, lane_sin_ref, high_ref, low_ref):
    chunks, _, wide = high_ref.shape
    tiles = wide // LANES
    lane_cos = lane_cos_ref[...]
    lane_sin = lane_sin_ref[...]
    for chunk in range(chunks):
        for tile in range(tiles):
            k = chunk * tiles + tile
            values = (
                base_cos_ref[:, k : k + 1] * lane_cos - base_sin_ref[:, k : k + 1] * lane_sin
            )
            high, low = split_high_low(values)
            high_ref[chunk, :, tile * LANES : (tile + 1) * LANES] = high
            low_ref[chunk, :, tile * LANES : (tile + 1) * LANES] = low


def fourier_table(row_waves, quarter_turns, chunks, lons, lon_count):
    tiles = -(-lons // LANES)
    offsets = (
        jnp.arange(chunks, dtype=jnp.int32)[:, None] * lons
        + jnp.arange(tiles, dtype=jnp.int32)[None, :] * LANES
    ).reshape(-1)
    factors = fourier_factors(row_waves, quarter_turns, offsets, lon_count)
    rows = row_waves.shape[0]
    tall = math.gcd(rows, 128)
    out = jax.ShapeDtypeStruct((chunks, rows, tiles * LANES), jnp.bfloat16)
    out_spec = pl.BlockSpec((chunks, tall, tiles * LANES), lambda i: (0, i, 0))
    size = chunks * rows * tiles * LANES
    return pl.pallas_call(
        wave_table_kernel,
        grid=(rows // tall,),
        in_specs=[pl.BlockSpec((tall, f.shape[1]), lambda i: (i, 0)) for f in factors],
        out_specs=[out_spec, out_spec],
        out_shape=[out, out],
        cost_estimate=pl.CostEstimate(flops=8 * size, bytes_accessed=4 * size, transcendentals=0),
        name="fourier_table",
    )(*factors)


def advect_kernel(
    tracer_ref, east_wind_ref, north_wind_ref, west_ref, east_ref, above_ref, below_ref, out_ref, pad_ref
):
    _, rows, columns = out_ref.shape
    tall, wide = pad_ref.shape
    centre = tracer_ref[0].astype(jnp.float32)
    pad_ref[:rows, :columns] = centre
    pad_ref[:rows, columns : columns + 1] = east_ref[0].astype(jnp.float32)
    pad_ref[:rows, wide - 1 : wide] = west_ref[0].astype(jnp.float32)
    pad_ref[rows : rows + 1, :columns] = below_ref[0]
    pad_ref[tall - 1 : tall, :columns] = above_ref[0]
    full = pad_ref[...]
    east_diff = (pltpu.roll(full, wide - 1, 1) - pltpu.roll(full, 1, 1))[:rows, :columns]
    north_diff = (pltpu.roll(full, tall - 1, 0) - pltpu.roll(full, 1, 0))[:rows, :columns]
    out_ref[0] = (
        centre
        - 0.5 * east_wind_ref[0].astype(jnp.float32) * east_diff
        - 0.5 * north_wind_ref[0].astype(jnp.float32) * north_diff
    )


def advect(tracer, east_wind, north_wind, first_row, lat_total):
    west, east = edges(tracer, GROUP, 2)
    above, below = edges(tracer, "lat", 1)
    levels, rows, columns = tracer.shape
    has_above = (first_row > 0).astype(jnp.float32)
    has_below = (first_row + rows < lat_total).astype(jnp.float32)
    above = above.astype(jnp.float32) * has_above
    below = below.astype(jnp.float32) * has_below
    block = pl.BlockSpec((1, rows, columns), lambda i: (i, 0, 0))
    column = pl.BlockSpec((1, rows, 1), lambda i: (i, 0, 0))
    line = pl.BlockSpec((1, 1, columns), lambda i: (i, 0, 0))
    size = levels * rows * columns
    return pl.pallas_call(
        advect_kernel,
        grid=(levels,),
        in_specs=[block, block, block, column, column, line, line],
        out_specs=block,
        out_shape=jax.ShapeDtypeStruct(tracer.shape, jnp.float32),
        scratch_shapes=[pltpu.VMEM((round_up(rows + 2, 8), round_up(columns + 2, 128)), jnp.float32)],
        cost_estimate=pl.CostEstimate(
            flops=10 * size, bytes_accessed=10 * size, transcendentals=0
        ),
        name="advect",
    )(tracer, east_wind, north_wind, west, east, above, below)


def split_high_low(values):
    high = values.astype(jnp.bfloat16)
    return high, (values - high.astype(jnp.float32)).astype(jnp.bfloat16)


def three_passes(high, low):
    return jnp.concatenate([high, high, low], axis=1)


def turned_passes(values):
    high, low = split_high_low(values.T)
    return jnp.concatenate([high, low, high], axis=0)


def fourier_kernel(
    rows_own, table_high_ref, table_low_ref, field_ref, wave_ref, keep_ref, out_ref, total_ref, pad_ref
):
    step = pl.program_id(0)
    _, levels, lat_rows, lons = field_ref.shape
    targets = out_ref.shape[0]
    rows_padded = table_high_ref.shape[1] // targets
    table = three_passes(table_high_ref[0], table_low_ref[0])

    @pl.when(step == 0)
    def _():
        pad_ref[...] = jnp.zeros_like(pad_ref)

    for level in range(levels):
        pad_ref[:lat_rows, :lons] = field_ref[0, level]
        term = jnp.dot(
            table, turned_passes(pad_ref[...]), preferred_element_type=jnp.float32
        )

        @pl.when(step == 0)
        def _():
            total_ref[level] = term

        @pl.when(step > 0)
        def _():
            total_ref[level] += term

    @pl.when(step == pl.num_programs(0) - 1)
    def _():
        kept = wave_ref[...] < keep_ref[...]
        for level in range(levels):
            masked = jnp.where(kept, total_ref[level][:, :lat_rows], 0.0)
            for target in range(targets):
                first = target * rows_padded
                out_ref[target, level * rows_own : (level + 1) * rows_own] = masked[
                    first : first + rows_own
                ]


def fourier_transform(table, field, row_waves, keep_m, targets, rows_own):
    chunks, levels, lat_rows, lons = field.shape
    rows = row_waves.shape[0]
    table_spec = pl.BlockSpec((1, rows, table[0].shape[2]), lambda i: (i, 0, 0))
    return pl.pallas_call(
        lambda *refs: fourier_kernel(rows_own, *refs),
        grid=(chunks,),
        in_specs=[
            table_spec,
            table_spec,
            pl.BlockSpec((1, levels, lat_rows, lons), lambda i: (i, 0, 0, 0)),
            pl.BlockSpec((rows, 1), lambda i: (0, 0)),
            pl.BlockSpec((1, lat_rows), lambda i: (0, 0)),
        ],
        out_specs=pl.BlockSpec((targets, levels * rows_own, lat_rows), lambda i: (0, 0, 0)),
        out_shape=jax.ShapeDtypeStruct((targets, levels * rows_own, lat_rows), jnp.float32),
        scratch_shapes=[
            pltpu.VMEM((levels, rows, round_up(lat_rows, LANES)), jnp.float32),
            pltpu.VMEM((round_up(lat_rows, LANES), table[0].shape[2]), jnp.float32),
        ],
        cost_estimate=pl.CostEstimate(
            flops=6 * rows * chunks * levels * lat_rows * lons,
            bytes_accessed=4 * rows * chunks * lons,
            transcendentals=0,
        ),
        name="fourier_transform",
    )(*table, field, row_waves[:, None], keep_m[None, :])


def legendre_setup(wave_ids, trunc_count, lat_total, lat_used, lat_padded):
    degree = jnp.minimum(wave_ids, trunc_count - 1).astype(jnp.float32)
    counter = jnp.arange(1, trunc_count, dtype=jnp.float32)
    log_terms = jnp.log1p(0.5 / counter)
    log_norm = jnp.sum(
        jnp.where(counter[None, :] <= degree[:, None], log_terms[None, :], 0.0), axis=1
    )
    rows = jnp.minimum(jnp.arange(lat_padded), lat_used - 1)
    colatitude = math.pi / lat_total * (rows.astype(jnp.float32) + 0.5)
    start_log = 0.5 * (log_norm[:, None] - math.log(2.0)) + degree[:, None] * jnp.log(
        jnp.sin(colatitude)
    )
    orders = jnp.arange(1, trunc_count + 1, dtype=jnp.float32)
    total = degree[:, None] + orders
    square = degree[:, None] * degree[:, None]
    growth = jnp.sqrt((4.0 * total * total - 1.0) / (total * total - square))
    lower = total - 1.0
    damping = jnp.sqrt(
        (lower * lower - square) / jnp.maximum(4.0 * lower * lower - 1.0, 1.0)
    )

    def blocked(values):
        return values.reshape(values.shape[0], -1, block_rows).transpose(1, 0, 2)

    return blocked(growth), blocked(damping), jnp.cos(colatitude)[None, :], start_log


def table_kernel(
    blocks_ref, growth_ref, damping_ref, cosine_ref, start_ref, high_ref, low_ref
):
    shape = start_ref.shape
    cosine = jnp.broadcast_to(cosine_ref[...], shape)
    slots = shape[0]
    wide = block_rows // 2 * slots

    def advance(index, carry):
        before, current, log_scale = carry
        scale = jnp.exp(log_scale)
        growth = growth_ref[index]
        damping = damping_ref[index]
        rows = []
        for offset in range(block_rows):
            rows.append(current * scale)
            advanced = growth[:, offset : offset + 1] * (
                cosine * current - damping[:, offset : offset + 1] * before
            )
            before, current = current, advanced
            if offset % 4 == 3:
                for parity in range(2):
                    pair = jnp.concatenate([rows[offset - 3 + parity], rows[offset - 1 + parity]])
                    high, low = split_high_low(pair)
                    first = pl.multiple_of(index * wide + offset // 4 * 2 * slots, 2 * slots)
                    high_ref[parity, 0, pl.ds(first, 2 * slots)] = high
                    low_ref[parity, 0, pl.ds(first, 2 * slots)] = low
        biggest = jnp.maximum(jnp.abs(before), jnp.abs(current))
        return before / biggest, current / biggest, log_scale + jnp.log(biggest)

    lax.fori_loop(
        0,
        blocks_ref[pl.program_id(0)] * (order_tile // block_rows),
        advance,
        (jnp.zeros(shape, jnp.float32), jnp.ones(shape, jnp.float32), start_ref[...]),
    )


def legendre_table(blocks_used, growth, damping, cosine, start_log):
    blocks, slots, _ = growth.shape
    lats = cosine.shape[1]
    rows = blocks * block_rows // 2 * slot_tile
    tiles = slots // slot_tile
    out = jax.ShapeDtypeStruct((2, tiles, rows, lats), jnp.bfloat16)
    coef_spec = pl.BlockSpec((blocks, slot_tile, block_rows), lambda i, used: (0, i, 0))
    out_spec = pl.BlockSpec((2, 1, rows, lats), lambda i, used: (0, i, 0, 0))
    size = 2 * tiles * rows * lats
    return pl.pallas_call(
        table_kernel,
        grid_spec=pltpu.PrefetchScalarGridSpec(
            num_scalar_prefetch=1,
            grid=(tiles,),
            in_specs=[
                coef_spec,
                coef_spec,
                pl.BlockSpec((1, lats), lambda i, used: (0, 0)),
                pl.BlockSpec((slot_tile, lats), lambda i, used: (i, 0)),
            ],
            out_specs=[out_spec, out_spec],
        ),
        out_shape=[out, out],
        cost_estimate=pl.CostEstimate(
            flops=10 * size, bytes_accessed=4 * size, transcendentals=size // 4
        ),
        name="legendre_table",
    )(blocks_used, growth, damping, cosine, start_log)


def contract_kernel(
    blocks_ref,
    high_ref,
    low_ref,
    folded_ref,
    own_ref,
    limit_ref,
    out_ref,
    weight_ref,
    sums_ref,
    mixed_ref,
):
    tile = pl.program_id(0)
    step = pl.program_id(1)
    rows = high_ref.shape[2]
    slots = own_ref.shape[0]
    orders = rows // slots
    _, lane_tiles, half, lanes = sums_ref.shape
    levels, rows_own, order_total = out_ref.shape

    @pl.when((tile == 0) & (step == 0))
    def _():
        sums_ref[...] = jnp.zeros_like(sums_ref)
        mixed_ref[...] = jnp.zeros_like(mixed_ref)
        for parity in range(2):
            weight_ref[parity] = turned_passes(folded_ref[parity])

    @pl.when(step < blocks_ref[tile])
    def _():
        own = own_ref[...] > 0.0
        for parity in range(2):
            full = jnp.dot(
                three_passes(high_ref[parity, 0], low_ref[parity, 0]),
                weight_ref[parity],
                preferred_element_type=jnp.float32,
            )
            picked = jnp.where(own[None], full.reshape(orders, slots, lane_tiles * lanes), 0.0)
            summed = jnp.sum(picked, axis=1)
            for k in range(lane_tiles):
                place = pl.ds(pl.multiple_of(step * orders, 8), orders)
                sums_ref[parity, k, place, :] += summed[:, k * lanes : (k + 1) * lanes]

    @pl.when((tile == pl.num_programs(0) - 1) & (step == pl.num_programs(1) - 1))
    def _():
        for parity in range(2):
            for k in range(lane_tiles):
                mixed_ref[k, pl.ds(parity, half, stride=2), :] = sums_ref[parity, k]
        turned = jnp.concatenate([mixed_ref[k].T for k in range(lane_tiles)], axis=0)
        turned = turned[:, :order_total]
        order = lax.broadcasted_iota(jnp.int32, turned.shape, 1)
        turned = jnp.where(order < limit_ref[...], turned, 0.0)
        for level in range(levels):
            out_ref[level] = turned[level * rows_own : (level + 1) * rows_own]


def contract_table(
    blocks_used, high, low, folded, own, limit, levels, rows_own
):
    _, tiles, rows, lats = high.shape
    columns = folded.shape[1]
    block = order_tile // 2 * slot_tile
    order_total = 2 * rows // slot_tile

    def table_map(i, j, used):
        return (0, i, jnp.maximum(jnp.minimum(j, used[i] - 1), 0), 0)

    table_spec = pl.BlockSpec((2, 1, block, lats), table_map)
    weight_spec = pl.BlockSpec((2, columns, lats), lambda i, j, used: (0, 0, 0))
    return pl.pallas_call(
        contract_kernel,
        grid_spec=pltpu.PrefetchScalarGridSpec(
            num_scalar_prefetch=1,
            grid=(tiles, rows // block),
            in_specs=[
                table_spec,
                table_spec,
                weight_spec,
                pl.BlockSpec((slot_tile, columns), lambda i, j, used: (i, 0)),
                pl.BlockSpec((columns, 1), lambda i, j, used: (0, 0)),
            ],
            out_specs=pl.BlockSpec((levels, rows_own, order_total), lambda i, j, used: (0, 0, 0)),
            scratch_shapes=[
                pltpu.VMEM((2, 3 * lats, columns), jnp.bfloat16),
                pltpu.VMEM((2, columns // LANES, order_total // 2, LANES), jnp.float32),
                pltpu.VMEM((columns // LANES, round_up(order_total, LANES), LANES), jnp.float32),
            ],
        ),
        out_shape=jax.ShapeDtypeStruct((levels, rows_own, order_total), jnp.float32),
        cost_estimate=pl.CostEstimate(
            flops=12 * tiles * rows * lats * columns,
            bytes_accessed=8 * tiles * rows * lats,
            transcendentals=0,
        ),
        name="legendre_contract",
    )(blocks_used, high, low, folded, own, limit)


def shards(tracer, wind_east, wind_north, keep_m, slot_wave):
    groups = lax.axis_size("lev") * lax.axis_size("fld")
    lat_parts = lax.axis_size("lat")
    levels, lat_rows, _ = tracer.shape
    own_levels = levels // groups
    slots_lat = slot_wave.shape[0] // lat_parts
    slots_own = -(-slots_lat // groups)
    first_row = lax.axis_index("lat") * lat_rows

    waves = jnp.pad(
        slot_wave.reshape(lat_parts, slots_lat),
        ((0, 0), (0, groups * slots_own - slots_lat)),
        constant_values=M,
    ).reshape(-1)
    place = lax.axis_index(("lat",) + GROUP) * slots_own
    my_waves = lax.dynamic_slice_in_dim(waves, place, slots_own)

    half_lat = NLAT // 2
    lat_padded = round_up(half_lat, 128)
    slots_padded = round_up(slots_own, slot_tile)
    index = jnp.arange(slots_own, dtype=jnp.int32)
    larger = (my_waves[None, :] > my_waves[:, None]) | (
        (my_waves[None, :] == my_waves[:, None]) & (index[None, :] < index[:, None])
    )
    row_of_slot = jnp.sum(larger.astype(jnp.int32), axis=1) + (slots_padded - slots_own)
    row_ids = jnp.arange(slots_padded, dtype=jnp.int32)
    placed = row_of_slot[None, :] == row_ids[:, None]
    padded_waves = M - jnp.sum(jnp.where(placed, M - my_waves[None, :], 0), axis=1)
    longest = jnp.max((M - padded_waves).reshape(-1, slot_tile), axis=1)
    blocks_used = jnp.maximum(-(-longest // order_tile), 0)
    table_high, table_low = legendre_table(
        blocks_used, *legendre_setup(padded_waves, M, NLAT, half_lat, lat_padded)
    )

    targets = lat_parts * groups
    rows_own = slots_own * 2
    rows_padded = round_up(rows_own, 8)
    row_waves = jnp.pad(
        jnp.repeat(waves.reshape(targets, slots_own), 2, axis=1),
        ((0, 0), (0, rows_padded - rows_own)),
        constant_values=M,
    ).reshape(-1)
    turns = jnp.arange(targets * rows_padded, dtype=jnp.int32) % 2
    table = fourier_table(row_waves, turns, groups, NLON // groups, NLON)

    advected = advect(tracer, wind_east, wind_north, first_row, NLAT)
    advected = lax.all_to_all(advected, GROUP, split_axis=0, concat_axis=0, tiled=True)
    advected = advected.reshape(groups, own_levels, lat_rows, -1)
    fourier = fourier_transform(table, advected, row_waves, keep_m, targets, rows_own)
    spectral_in = lax.all_to_all(
        fourier, ("lat",) + GROUP, split_axis=0, concat_axis=0, tiled=True
    )
    used = levels * rows_own
    weighted = spectral_in.reshape(lat_parts, used, lat_rows).transpose(1, 0, 2)
    weighted = weighted.reshape(used, NLAT)
    sines = jnp.sin(math.pi / NLAT * (jnp.arange(NLAT, dtype=jnp.float32) + 0.5))
    weighted = weighted * (sines * math.sqrt(2.0 / NLAT))[None, :]
    north = weighted[:, :half_lat]
    south = jnp.flip(weighted[:, half_lat:], axis=1)
    columns = round_up(used, 128)
    folded = jnp.pad(
        jnp.stack([north + south, north - south]),
        ((0, 0), (0, columns - used), (0, lat_padded - half_lat)),
    )
    slot_of_column = jnp.arange(columns, dtype=jnp.int32) % rows_own // 2
    column_of_row = slot_of_column[None, :, None] == index[None, None, :]
    own = jnp.any(column_of_row & placed[:, None, :], axis=2).astype(jnp.float32)
    limit = jnp.sum(jnp.where(column_of_row[0], M - my_waves[None, :], 0), axis=1)[:, None]
    result = contract_table(
        blocks_used, table_high, table_low, folded, own, limit, levels, rows_own
    )
    result = lax.all_to_all(result, GROUP, split_axis=0, concat_axis=0, tiled=True)
    result = result.reshape(groups, own_levels, slots_own, 2, M).transpose(1, 0, 2, 3, 4)
    return result.reshape(own_levels, groups * slots_own, 2, M)[:, :slots_lat]


def solution(mesh):
    return jax.shard_map(
        shards,
        mesh=mesh,
        in_specs=(
            P("member", "lat", ("lev", "fld")),
            P("member", "lat", ("lev", "fld")),
            P("member", "lat", ("lev", "fld")),
            P("lat"),
            P(),
        ),
        out_specs=P(("member", "lev", "fld"), "lat", None, None),
        check_vma=False,
    )
```

```python
import math

import jax
import jax.numpy as jnp
from jax import lax
from jax.experimental import pallas as pl
from jax.experimental.pallas import tpu as pltpu
from jax.sharding import PartitionSpec as P

M = 400
NLAT = 800
NLON = 1600

block_rows = 16
slot_tile = 8
order_tile = 80
LANES = 128
GROUP = ("lev", "fld")


def round_up(value, multiple):
    return -(-value // multiple) * multiple


def edges(block, axis, dim):
    count = lax.axis_size(axis)
    forward = [(i, (i + 1) % count) for i in range(count)]
    backward = [(target, source) for source, target in forward]
    low = lax.ppermute(
        lax.slice_in_dim(block, block.shape[dim] - 1, None, axis=dim), axis, forward
    )
    high = lax.ppermute(lax.slice_in_dim(block, 0, 1, axis=dim), axis, backward)
    return low, high


def fourier_factors(row_waves, quarter_turns, offsets, lon_count):
    step = 2.0 * math.pi / lon_count
    lane = row_waves[:, None] * jnp.arange(LANES, dtype=jnp.int32)[None, :] % lon_count
    lane = step * lane.astype(jnp.float32)
    shift = quarter_turns * (lon_count // 4)
    base = (offsets[:, None] * row_waves[None, :] + shift[None, :]) % lon_count
    base = step * base.astype(jnp.float32)
    factor = 1.0 / math.sqrt(lon_count)
    return (jnp.cos(base) * factor).T, (jnp.sin(base) * factor).T, jnp.cos(lane), jnp.sin(lane)


def wave_table_kernel(base_cos_ref, base_sin_ref, lane_cos_ref, lane_sin_ref, high_ref, low_ref):
    chunks, _, wide = high_ref.shape
    tiles = wide // LANES
    lane_cos = lane_cos_ref[...]
    lane_sin = lane_sin_ref[...]
    for chunk in range(chunks):
        for tile in range(tiles):
            k = chunk * tiles + tile
            values = (
                base_cos_ref[:, k : k + 1] * lane_cos - base_sin_ref[:, k : k + 1] * lane_sin
            )
            high, low = split_high_low(values)
            high_ref[chunk, :, tile * LANES : (tile + 1) * LANES] = high
            low_ref[chunk, :, tile * LANES : (tile + 1) * LANES] = low


def fourier_table(row_waves, quarter_turns, chunks, lons, lon_count):
    tiles = -(-lons // LANES)
    offsets = (
        jnp.arange(chunks, dtype=jnp.int32)[:, None] * lons
        + jnp.arange(tiles, dtype=jnp.int32)[None, :] * LANES
    ).reshape(-1)
    factors = fourier_factors(row_waves, quarter_turns, offsets, lon_count)
    rows = row_waves.shape[0]
    tall = math.gcd(rows, 128)
    out = jax.ShapeDtypeStruct((chunks, rows, tiles * LANES), jnp.bfloat16)
    out_spec = pl.BlockSpec((chunks, tall, tiles * LANES), lambda i: (0, i, 0))
    size = chunks * rows * tiles * LANES
    return pl.pallas_call(
        wave_table_kernel,
        grid=(rows // tall,),
        in_specs=[pl.BlockSpec((tall, f.shape[1]), lambda i: (i, 0)) for f in factors],
        out_specs=[out_spec, out_spec],
        out_shape=[out, out],
        cost_estimate=pl.CostEstimate(flops=8 * size, bytes_accessed=4 * size, transcendentals=0),
        name="fourier_table",
    )(*factors)


def advect_kernel(
    tracer_ref, east_wind_ref, north_wind_ref, west_ref, east_ref, above_ref, below_ref, out_ref, pad_ref
):
    _, rows, columns = out_ref.shape
    tall, wide = pad_ref.shape
    centre = tracer_ref[0].astype(jnp.float32)
    pad_ref[:rows, :columns] = centre
    pad_ref[:rows, columns : columns + 1] = east_ref[0].astype(jnp.float32)
    pad_ref[:rows, wide - 1 : wide] = west_ref[0].astype(jnp.float32)
    pad_ref[rows : rows + 1, :columns] = below_ref[0]
    pad_ref[tall - 1 : tall, :columns] = above_ref[0]
    full = pad_ref[...]
    east_diff = (pltpu.roll(full, wide - 1, 1) - pltpu.roll(full, 1, 1))[:rows, :columns]
    north_diff = (pltpu.roll(full, tall - 1, 0) - pltpu.roll(full, 1, 0))[:rows, :columns]
    out_ref[0] = (
        centre
        - 0.5 * east_wind_ref[0].astype(jnp.float32) * east_diff
        - 0.5 * north_wind_ref[0].astype(jnp.float32) * north_diff
    )


def advect(tracer, east_wind, north_wind, first_row, lat_total):
    west, east = edges(tracer, GROUP, 2)
    above, below = edges(tracer, "lat", 1)
    levels, rows, columns = tracer.shape
    has_above = (first_row > 0).astype(jnp.float32)
    has_below = (first_row + rows < lat_total).astype(jnp.float32)
    above = above.astype(jnp.float32) * has_above
    below = below.astype(jnp.float32) * has_below
    block = pl.BlockSpec((1, rows, columns), lambda i: (i, 0, 0))
    column = pl.BlockSpec((1, rows, 1), lambda i: (i, 0, 0))
    line = pl.BlockSpec((1, 1, columns), lambda i: (i, 0, 0))
    size = levels * rows * columns
    return pl.pallas_call(
        advect_kernel,
        grid=(levels,),
        in_specs=[block, block, block, column, column, line, line],
        out_specs=block,
        out_shape=jax.ShapeDtypeStruct(tracer.shape, jnp.float32),
        scratch_shapes=[pltpu.VMEM((round_up(rows + 2, 8), round_up(columns + 2, 128)), jnp.float32)],
        cost_estimate=pl.CostEstimate(
            flops=10 * size, bytes_accessed=10 * size, transcendentals=0
        ),
        name="advect",
    )(tracer, east_wind, north_wind, west, east, above, below)


def split_high_low(values):
    high = values.astype(jnp.bfloat16)
    return high, (values - high.astype(jnp.float32)).astype(jnp.bfloat16)


def three_passes(high, low):
    return jnp.concatenate([high, high, low], axis=1)


def turned_passes(values):
    high, low = split_high_low(values.T)
    return jnp.concatenate([high, low, high], axis=0)


def fourier_kernel(
    rows_own, table_high_ref, table_low_ref, field_ref, wave_ref, keep_ref, out_ref, total_ref, pad_ref
):
    step = pl.program_id(0)
    _, levels, lat_rows, lons = field_ref.shape
    targets = out_ref.shape[0]
    rows_padded = table_high_ref.shape[1] // targets
    table = three_passes(table_high_ref[0], table_low_ref[0])

    @pl.when(step == 0)
    def _():
        pad_ref[...] = jnp.zeros_like(pad_ref)

    for level in range(levels):
        pad_ref[:lat_rows, :lons] = field_ref[0, level]
        term = jnp.dot(
            table, turned_passes(pad_ref[...]), preferred_element_type=jnp.float32
        )

        @pl.when(step == 0)
        def _():
            total_ref[level] = term

        @pl.when(step > 0)
        def _():
            total_ref[level] += term

    @pl.when(step == pl.num_programs(0) - 1)
    def _():
        kept = wave_ref[...] < keep_ref[...]
        for level in range(levels):
            masked = jnp.where(kept, total_ref[level][:, :lat_rows], 0.0)
            for target in range(targets):
                first = target * rows_padded
                out_ref[target, level * rows_own : (level + 1) * rows_own] = masked[
                    first : first + rows_own
                ]


def fourier_transform(table, field, row_waves, keep_m, targets, rows_own):
    chunks, levels, lat_rows, lons = field.shape
    rows = row_waves.shape[0]
    table_spec = pl.BlockSpec((1, rows, table[0].shape[2]), lambda i: (i, 0, 0))
    return pl.pallas_call(
        lambda *refs: fourier_kernel(rows_own, *refs),
        grid=(chunks,),
        in_specs=[
            table_spec,
            table_spec,
            pl.BlockSpec((1, levels, lat_rows, lons), lambda i: (i, 0, 0, 0)),
            pl.BlockSpec((rows, 1), lambda i: (0, 0)),
            pl.BlockSpec((1, lat_rows), lambda i: (0, 0)),
        ],
        out_specs=pl.BlockSpec((targets, levels * rows_own, lat_rows), lambda i: (0, 0, 0)),
        out_shape=jax.ShapeDtypeStruct((targets, levels * rows_own, lat_rows), jnp.float32),
        scratch_shapes=[
            pltpu.VMEM((levels, rows, round_up(lat_rows, LANES)), jnp.float32),
            pltpu.VMEM((round_up(lat_rows, LANES), table[0].shape[2]), jnp.float32),
        ],
        cost_estimate=pl.CostEstimate(
            flops=6 * rows * chunks * levels * lat_rows * lons,
            bytes_accessed=4 * rows * chunks * lons,
            transcendentals=0,
        ),
        name="fourier_transform",
    )(*table, field, row_waves[:, None], keep_m[None, :])


def legendre_setup(wave_ids, trunc_count, lat_total, lat_used, lat_padded):
    degree = jnp.minimum(wave_ids, trunc_count - 1).astype(jnp.float32)
    counter = jnp.arange(1, trunc_count, dtype=jnp.float32)
    log_terms = jnp.log1p(0.5 / counter)
    log_norm = jnp.sum(
        jnp.where(counter[None, :] <= degree[:, None], log_terms[None, :], 0.0), axis=1
    )
    rows = jnp.minimum(jnp.arange(lat_padded), lat_used - 1)
    colatitude = math.pi / lat_total * (rows.astype(jnp.float32) + 0.5)
    start_log = 0.5 * (log_norm[:, None] - math.log(2.0)) + degree[:, None] * jnp.log(
        jnp.sin(colatitude)
    )
    orders = jnp.arange(1, trunc_count + 1, dtype=jnp.float32)
    total = degree[:, None] + orders
    square = degree[:, None] * degree[:, None]
    growth = jnp.sqrt((4.0 * total * total - 1.0) / (total * total - square))
    lower = total - 1.0
    damping = jnp.sqrt(
        (lower * lower - square) / jnp.maximum(4.0 * lower * lower - 1.0, 1.0)
    )

    def blocked(values):
        return values.reshape(values.shape[0], -1, block_rows).transpose(1, 0, 2)

    return blocked(growth), blocked(damping), jnp.cos(colatitude)[None, :], start_log


def table_kernel(
    blocks_ref, growth_ref, damping_ref, cosine_ref, start_ref, table_ref
):
    shape = start_ref.shape
    cosine = jnp.broadcast_to(cosine_ref[...], shape)
    slots = shape[0]
    wide = block_rows // 2 * slots

    def advance(index, carry):
        before, current, log_scale = carry
        scale = jnp.exp(log_scale)
        growth = growth_ref[index]
        damping = damping_ref[index]
        for offset in range(block_rows):
            first = pl.multiple_of(index * wide + offset // 2 * slots, slots)
            table_ref[offset % 2, 0, pl.ds(first, slots)] = current * scale
            advanced = growth[:, offset : offset + 1] * (
                cosine * current - damping[:, offset : offset + 1] * before
            )
            before, current = current, advanced
        biggest = jnp.maximum(jnp.abs(before), jnp.abs(current))
        return before / biggest, current / biggest, log_scale + jnp.log(biggest)

    lax.fori_loop(
        0,
        blocks_ref[pl.program_id(0)] * (order_tile // block_rows),
        advance,
        (jnp.zeros(shape, jnp.float32), jnp.ones(shape, jnp.float32), start_ref[...]),
    )


def legendre_table(blocks_used, growth, damping, cosine, start_log):
    blocks, slots, _ = growth.shape
    lats = cosine.shape[1]
    rows = blocks * block_rows // 2 * slot_tile
    tiles = slots // slot_tile
    out = jax.ShapeDtypeStruct((2, tiles, rows, lats), jnp.float32)
    coef_spec = pl.BlockSpec((blocks, slot_tile, block_rows), lambda i, used: (0, i, 0))
    out_spec = pl.BlockSpec((2, 1, rows, lats), lambda i, used: (0, i, 0, 0))
    size = 2 * tiles * rows * lats
    return pl.pallas_call(
        table_kernel,
        grid_spec=pltpu.PrefetchScalarGridSpec(
            num_scalar_prefetch=1,
            grid=(tiles,),
            in_specs=[
                coef_spec,
                coef_spec,
                pl.BlockSpec((1, lats), lambda i, used: (0, 0)),
                pl.BlockSpec((slot_tile, lats), lambda i, used: (i, 0)),
            ],
            out_specs=out_spec,
        ),
        out_shape=out,
        cost_estimate=pl.CostEstimate(
            flops=10 * size, bytes_accessed=4 * size, transcendentals=size // 4
        ),
        name="legendre_table",
    )(blocks_used, growth, damping, cosine, start_log)


def contract_kernel(
    blocks_ref,
    table_ref,
    folded_ref,
    own_ref,
    limit_ref,
    out_ref,
    weight_ref,
    sums_ref,
    mixed_ref,
):
    tile = pl.program_id(0)
    step = pl.program_id(1)
    rows = table_ref.shape[2]
    slots = own_ref.shape[0]
    orders = rows // slots
    _, lane_tiles, half, lanes = sums_ref.shape
    levels, rows_own, order_total = out_ref.shape

    @pl.when((tile == 0) & (step == 0))
    def _():
        sums_ref[...] = jnp.zeros_like(sums_ref)
        mixed_ref[...] = jnp.zeros_like(mixed_ref)
        for parity in range(2):
            weight_ref[parity] = turned_passes(folded_ref[parity])

    @pl.when(step < blocks_ref[tile])
    def _():
        own = own_ref[...] > 0.0
        for parity in range(2):
            full = jnp.dot(
                three_passes(*split_high_low(table_ref[parity, 0])),
                weight_ref[parity],
                preferred_element_type=jnp.float32,
            )
            picked = jnp.where(own[None], full.reshape(orders, slots, lane_tiles * lanes), 0.0)
            summed = jnp.sum(picked, axis=1)
            for k in range(lane_tiles):
                place = pl.ds(pl.multiple_of(step * orders, 8), orders)
                sums_ref[parity, k, place, :] += summed[:, k * lanes : (k + 1) * lanes]

    @pl.when((tile == pl.num_programs(0) - 1) & (step == pl.num_programs(1) - 1))
    def _():
        for parity in range(2):
            for k in range(lane_tiles):
                mixed_ref[k, pl.ds(parity, half, stride=2), :] = sums_ref[parity, k]
        turned = jnp.concatenate([mixed_ref[k].T for k in range(lane_tiles)], axis=0)
        turned = turned[:, :order_total]
        order = lax.broadcasted_iota(jnp.int32, turned.shape, 1)
        turned = jnp.where(order < limit_ref[...], turned, 0.0)
        for level in range(levels):
            out_ref[level] = turned[level * rows_own : (level + 1) * rows_own]


def contract_table(
    blocks_used, table, folded, own, limit, levels, rows_own
):
    _, tiles, rows, lats = table.shape
    columns = folded.shape[1]
    block = order_tile // 2 * slot_tile
    order_total = 2 * rows // slot_tile

    def table_map(i, j, used):
        return (0, i, jnp.maximum(jnp.minimum(j, used[i] - 1), 0), 0)

    table_spec = pl.BlockSpec((2, 1, block, lats), table_map)
    weight_spec = pl.BlockSpec((2, columns, lats), lambda i, j, used: (0, 0, 0))
    return pl.pallas_call(
        contract_kernel,
        grid_spec=pltpu.PrefetchScalarGridSpec(
            num_scalar_prefetch=1,
            grid=(tiles, rows // block),
            in_specs=[
                table_spec,
                weight_spec,
                pl.BlockSpec((slot_tile, columns), lambda i, j, used: (i, 0)),
                pl.BlockSpec((columns, 1), lambda i, j, used: (0, 0)),
            ],
            out_specs=pl.BlockSpec((levels, rows_own, order_total), lambda i, j, used: (0, 0, 0)),
            scratch_shapes=[
                pltpu.VMEM((2, 3 * lats, columns), jnp.bfloat16),
                pltpu.VMEM((2, columns // LANES, order_total // 2, LANES), jnp.float32),
                pltpu.VMEM((columns // LANES, round_up(order_total, LANES), LANES), jnp.float32),
            ],
        ),
        out_shape=jax.ShapeDtypeStruct((levels, rows_own, order_total), jnp.float32),
        cost_estimate=pl.CostEstimate(
            flops=12 * tiles * rows * lats * columns,
            bytes_accessed=8 * tiles * rows * lats,
            transcendentals=0,
        ),
        name="legendre_contract",
    )(blocks_used, table, folded, own, limit)


def shards(tracer, wind_east, wind_north, keep_m, slot_wave):
    groups = lax.axis_size("lev") * lax.axis_size("fld")
    lat_parts = lax.axis_size("lat")
    levels, lat_rows, _ = tracer.shape
    own_levels = levels // groups
    slots_lat = slot_wave.shape[0] // lat_parts
    slots_own = -(-slots_lat // groups)
    first_row = lax.axis_index("lat") * lat_rows

    waves = jnp.pad(
        slot_wave.reshape(lat_parts, slots_lat),
        ((0, 0), (0, groups * slots_own - slots_lat)),
        constant_values=M,
    ).reshape(-1)
    place = lax.axis_index(("lat",) + GROUP) * slots_own
    my_waves = lax.dynamic_slice_in_dim(waves, place, slots_own)

    half_lat = NLAT // 2
    lat_padded = round_up(half_lat, 128)
    slots_padded = round_up(slots_own, slot_tile)
    index = jnp.arange(slots_own, dtype=jnp.int32)
    larger = (my_waves[None, :] > my_waves[:, None]) | (
        (my_waves[None, :] == my_waves[:, None]) & (index[None, :] < index[:, None])
    )
    row_of_slot = jnp.sum(larger.astype(jnp.int32), axis=1) + (slots_padded - slots_own)
    row_ids = jnp.arange(slots_padded, dtype=jnp.int32)
    placed = row_of_slot[None, :] == row_ids[:, None]
    padded_waves = M - jnp.sum(jnp.where(placed, M - my_waves[None, :], 0), axis=1)
    longest = jnp.max((M - padded_waves).reshape(-1, slot_tile), axis=1)
    blocks_used = jnp.maximum(-(-longest // order_tile), 0)
    legendre = legendre_table(
        blocks_used, *legendre_setup(padded_waves, M, NLAT, half_lat, lat_padded)
    )

    targets = lat_parts * groups
    rows_own = slots_own * 2
    rows_padded = round_up(rows_own, 8)
    row_waves = jnp.pad(
        jnp.repeat(waves.reshape(targets, slots_own), 2, axis=1),
        ((0, 0), (0, rows_padded - rows_own)),
        constant_values=M,
    ).reshape(-1)
    turns = jnp.arange(targets * rows_padded, dtype=jnp.int32) % 2
    table = fourier_table(row_waves, turns, groups, NLON // groups, NLON)

    advected = advect(tracer, wind_east, wind_north, first_row, NLAT)
    advected = lax.all_to_all(advected, GROUP, split_axis=0, concat_axis=0, tiled=True)
    advected = advected.reshape(groups, own_levels, lat_rows, -1)
    fourier = fourier_transform(table, advected, row_waves, keep_m, targets, rows_own)
    spectral_in = lax.all_to_all(
        fourier, ("lat",) + GROUP, split_axis=0, concat_axis=0, tiled=True
    )
    used = levels * rows_own
    weighted = spectral_in.reshape(lat_parts, used, lat_rows).transpose(1, 0, 2)
    weighted = weighted.reshape(used, NLAT)
    sines = jnp.sin(math.pi / NLAT * (jnp.arange(NLAT, dtype=jnp.float32) + 0.5))
    weighted = weighted * (sines * math.sqrt(2.0 / NLAT))[None, :]
    north = weighted[:, :half_lat]
    south = jnp.flip(weighted[:, half_lat:], axis=1)
    columns = round_up(used, 128)
    folded = jnp.pad(
        jnp.stack([north + south, north - south]),
        ((0, 0), (0, columns - used), (0, lat_padded - half_lat)),
    )
    slot_of_column = jnp.arange(columns, dtype=jnp.int32) % rows_own // 2
    column_of_row = slot_of_column[None, :, None] == index[None, None, :]
    own = jnp.any(column_of_row & placed[:, None, :], axis=2).astype(jnp.float32)
    limit = jnp.sum(jnp.where(column_of_row[0], M - my_waves[None, :], 0), axis=1)[:, None]
    result = contract_table(
        blocks_used, legendre, folded, own, limit, levels, rows_own
    )
    result = lax.all_to_all(result, GROUP, split_axis=0, concat_axis=0, tiled=True)
    result = result.reshape(groups, own_levels, slots_own, 2, M).transpose(1, 0, 2, 3, 4)
    return result.reshape(own_levels, groups * slots_own, 2, M)[:, :slots_lat]


def solution(mesh):
    return jax.shard_map(
        shards,
        mesh=mesh,
        in_specs=(
            P("member", "lat", ("lev", "fld")),
            P("member", "lat", ("lev", "fld")),
            P("member", "lat", ("lev", "fld")),
            P("lat"),
            P(),
        ),
        out_specs=P(("member", "lev", "fld"), "lat", None, None),
        check_vma=False,
    )
```
